256 devices in a mesh: gx: 8 (over z), gy: 4 (over y), gz: 8 (over x, core).
Axes of the slice: x: 4, y: 4, z: 8, core: 2. Of those that a mesh axis runs over, the one named last changes fastest.
Arguments:
- distribution: bfloat16 [16, 32, 64, 12, 512], P('gx', 'gy', 'gz'), may hold values from 0.019897461 to 1
- block_ids: int32 [16, 32, 64, 12], P('gx', 'gy', 'gz'), may hold values from 0 to 215, as said below
- cell_counts: int32 [16, 32, 64], P('gx', 'gy', 'gz'), may hold values from 6 to 12
- owner: int32 [16, 32, 64], P('gx', 'gy', 'gz'), may hold values from 0 to 63, as said below
- restitution: bfloat16 [16, 32, 64], P('gx', 'gy', 'gz'), may hold values from 0.5 to 0.94921875
Outputs:
- moved_distribution: bfloat16 [4, 8192, 12, 512], P('gy', ('gx', 'gz'))
- moved_ids: int32 [4, 8192, 12], P('gy', ('gx', 'gz'))
- moved_counts: int32 [4, 8192], P('gy', ('gx', 'gz'))
The draws below stay inside these ranges and needn't reach their ends.
Inputs may be any that keep to these rules, and one draw needn't show every extreme that they name: `block_ids`: the 12 numbers of one cell are distinct block numbers. `owner`: owner g means the device of the cell's gy row with gx index g // 8 and gz index g % 8. Each device sends exactly 2 of its cells to each of the 64 devices of its gy row (itself included), and each device owns exactly 128 cells afterwards.
All inputs are finite; a program needn't handle non-finite values.
Results may differ from the reference program's by a relative error of at most 0.001.
The reference program's roundings to bfloat16 on the way (of `read` and `relaxed`) count: a program that leaves them out, or rounds other values in their place, can miss the bound.
Values may be sent and summed in bfloat16 or wider, within the bound.
No kernel may reach another device: no remote copies, remote signals or barrier semaphores. Data moves between devices by JAX's collectives and lax.ppermute only.
A program may use at most 64 MiB of HBM per device.

```python
import math
import jax
import jax.numpy as jnp
import numpy as np
from jax import lax

NV1 = 48
BLK = 8
MAXB = 12
CX = 2
CY = 8
CZ = 8
VB = 512
CELLS = 128
NX = 16
NY = 32
NZ = 64
GROUP = 64
CAPS = 2
N_GX = 8
N_GY = 4
N_GZ = 8


def neighbour_table():
    entries = []
    for first in (-1, 0, 1):
        for second in (-1, 0, 1):
            for third in (-1, 0, 1):
                if first != 0 or second != 0 or third != 0:
                    entries.append((first, second, third))
    return np.array(entries, dtype=np.int32)


def draw_block_ids(key, part):
    blocks_edge = NV1 // BLK
    total_cells = NX * NY * NZ
    first_key, second_key = jax.random.split(jax.random.fold_in(key, 11))
    centers = jax.random.randint(first_key, (total_cells, 3), 1, blocks_edge - 1)
    centers = centers.at[0].set(jnp.ones((3,), jnp.int32))
    centers = centers.at[total_cells - 1].set(jnp.full((3,), blocks_edge - 2, jnp.int32))
    scores = jax.random.randint(second_key, (total_cells, 26), 0, 1 << 20) * 32 + jnp.arange(26, dtype=jnp.int32)
    scores = scores.at[0, 0].set(-1)
    scores = scores.at[total_cells - 1, 25].set(-1)
    ordering = jnp.argsort(scores, axis=-1)[..., :MAXB - 1]
    offset_table = jnp.asarray(neighbour_table())
    chosen = offset_table[ordering]
    coords = jnp.concatenate([centers[..., None, :], centers[..., None, :] + chosen], axis=-2)
    ids = (coords[..., 0] * blocks_edge + coords[..., 1]) * blocks_edge + coords[..., 2]
    return ids.reshape(NX, NY, NZ, MAXB).astype(jnp.int32)


def draw_cell_counts(key, part):
    first_key, second_key = jax.random.split(jax.random.fold_in(key, 23))
    drawn = jax.random.randint(first_key, (NX * NY * NZ,), MAXB // 2, MAXB + 1)
    chosen_cell = jax.random.randint(second_key, (), 0, NX * NY * NZ)
    drawn = drawn.at[chosen_cell].set(MAXB)
    return drawn.reshape(NX, NY, NZ).astype(jnp.int32)


def draw_owner(key, part):
    first_key, second_key = jax.random.split(jax.random.fold_in(key, 37))
    rotation = jax.vmap(lambda one_key: jax.random.permutation(one_key, GROUP))(jax.random.split(first_key, N_GY))
    inverse = jnp.argsort(rotation, axis=1)
    placement = jax.vmap(lambda one_key: jax.random.permutation(one_key, CELLS))(jax.random.split(second_key, N_GY * GROUP))
    placement = placement.reshape(N_GY, GROUP, CELLS)
    step_count = placement // CAPS
    shifted = (rotation[:, :, None] + step_count) % GROUP
    destination_holder = jnp.take_along_axis(inverse[:, None, :], shifted.reshape(N_GY, 1, GROUP * CELLS), axis=2)
    destination_holder = destination_holder.reshape(N_GY, N_GX, N_GZ, CX, CY, CZ)
    destination_holder = destination_holder.transpose((1, 3, 0, 4, 2, 5)).reshape(NX, NY, NZ)
    return destination_holder.astype(jnp.int32)


def shard_levels(own_key, shape, cuts, smallest, top_value):
    def one(position, parts):
        draws = jax.random.uniform(jax.random.fold_in(jax.random.fold_in(own_key, 6), position), (parts,), jnp.float32, smallest / len(cuts), top_value / len(cuts))
        return jnp.repeat(jnp.exp(draws), shape[position] // parts).reshape((-1,) + (1,) * (len(shape) - position - 1))

    level = one(*cuts[0])
    for cut in cuts[1:]:
        level = level * one(*cut)
    return level


def setup_inputs(seed: int = 0) -> dict:
    keys = jax.random.split(jax.random.key(seed), 6)
    return {
        "distribution": jnp.clip(jnp.exp(math.log(1.0) - 3.9171631 * jax.random.uniform(keys[0], (NX, NY, NZ, MAXB, VB), jnp.float32) ** shard_levels(keys[0], (NX, NY, NZ, MAXB, VB), ((0, 8), (1, 4), (2, 8)), -0.2, 0.2)), 0.019897461, 1.0).astype(jnp.bfloat16),
        "block_ids": draw_block_ids(jax.random.fold_in(keys[5], 71), 0),
        "cell_counts": draw_cell_counts(jax.random.fold_in(keys[5], 71), 0),
        "owner": draw_owner(jax.random.fold_in(keys[5], 71), 0),
        "restitution": jnp.clip(0.5 + 0.44921875 * jax.random.uniform(keys[4], (NX, NY, NZ), jnp.float32) ** shard_levels(keys[4], (NX, NY, NZ), ((0, 8), (1, 4), (2, 8)), -0.2, 0.2), 0.5, 0.94921875).astype(jnp.bfloat16),
    }


STEP_COEFF = 0.6
IMPACT_KIND = 0.02

def inner_offsets():
    velocity_index = jnp.arange(BLK ** 3, dtype=jnp.int32)
    coords = jnp.stack([velocity_index // (BLK * BLK), velocity_index // BLK % BLK, velocity_index % BLK])
    return coords.astype(jnp.float32) - (BLK - 1) / 2.0

def block_centers(ids):
    blocks_edge = NV1 // BLK
    coords = jnp.stack([ids // (blocks_edge * blocks_edge), ids // blocks_edge % blocks_edge, ids % blocks_edge])
    return coords.astype(jnp.float32) * BLK + (BLK - 1) / 2.0 - (NV1 - 1) / 2.0

def neighbor_values(own_ids, other_ids, other_values):
    matches = ((own_ids[..., :, None] == other_ids[..., None, :]) & (own_ids[..., :, None] >= 0)).astype(jnp.int32)
    chosen = jnp.argmax(matches, axis=-1).astype(jnp.int32)
    found_any = lax.optimization_barrier(jnp.max(matches, axis=-1)).astype(jnp.float32)
    picked = jnp.take_along_axis(other_values, chosen[..., None], axis=-2).astype(jnp.float32)
    return picked * found_any[..., None]

def transport(values, raw_ids, own_ids, live_mask, neighbours):
    inner_offset = inner_offsets()
    centers = block_centers(raw_ids)
    center_value = values.astype(jnp.float32)
    flux_sum = jnp.zeros(center_value.shape, jnp.float32)
    lam = STEP_COEFF / (NV1 - 1)
    for direction in range(3):
        lower_vals, lower_ids, upper_vals, upper_ids = neighbours[direction]
        velocity = centers[direction][..., None] + inner_offset[direction]
        from_lower = neighbor_values(own_ids, lower_ids, lower_vals)
        from_upper = neighbor_values(own_ids, upper_ids, upper_vals)
        flux_sum = flux_sum + jnp.maximum(velocity, 0.0) * (center_value - from_lower) + jnp.minimum(velocity, 0.0) * (from_upper - center_value)
    return ((center_value - lam * flux_sum) * live_mask[..., None]).astype(jnp.bfloat16)

def relax(read, raw_ids, live_mask, coefficient):
    inner_offset = inner_offsets()
    centers = block_centers(raw_ids)
    tile_span = inner_offset.shape[1]
    squares = lax.optimization_barrier(jnp.sum(inner_offset * inner_offset, axis=0))
    weights_table = jnp.concatenate([jnp.ones((1, tile_span), jnp.float32), inner_offset, squares[None]], axis=0).T.astype(jnp.bfloat16)
    leading = read.shape[:-1]
    block_sums = jnp.dot(read.reshape(-1, tile_span), weights_table, preferred_element_type=jnp.float32).reshape(leading + (5,))
    block_mass = block_sums[..., 0]
    particle_count_field = lax.optimization_barrier(jnp.sum(block_mass, axis=-1))
    momentum = [lax.optimization_barrier(jnp.sum(block_mass * centers[k] + block_sums[..., 1 + k], axis=-1)) for k in range(3)]
    center_sq = centers[0] * centers[0] + centers[1] * centers[1] + centers[2] * centers[2]
    cross = centers[0] * block_sums[..., 1] + centers[1] * block_sums[..., 2] + centers[2] * block_sums[..., 3]
    motion_work_sum = lax.optimization_barrier(jnp.sum(block_mass * center_sq + 2.0 * cross + block_sums[..., 4], axis=-1))
    average_drift = [momentum[k] / particle_count_field for k in range(3)]
    thermal_spread = (motion_work_sum / particle_count_field - (average_drift[0] * average_drift[0] + average_drift[1] * average_drift[1] + average_drift[2] * average_drift[2])) / 3.0
    return_parcels_home = coefficient.astype(jnp.float32)
    destination_holder = thermal_spread * (1.0 + return_parcels_home) * (1.0 + return_parcels_home) / 4.0
    equilibration_frequency = 1.0 - jnp.exp(-IMPACT_KIND * (particle_count_field / tile_span) * jnp.sqrt(thermal_spread))
    distance = jnp.zeros(read.shape, jnp.float32)
    for k in range(3):
        offset_k = centers[k][..., None] + inner_offset[k] - average_drift[k][..., None, None]
        distance = distance + offset_k * offset_k
    scale = particle_count_field / (2.0 * math.pi * destination_holder) ** 1.5
    maxwellian = scale[..., None, None] * jnp.exp(-distance / (2.0 * destination_holder[..., None, None]))
    stream_vals = read.astype(jnp.float32)
    relaxed = (stream_vals + equilibration_frequency[..., None, None] * (maxwellian - stream_vals)) * live_mask[..., None]
    return relaxed.astype(jnp.bfloat16)

def to_groups(array):
    trailing = array.shape[3:]
    shaped = array.reshape((N_GX, CX, N_GY, CY, N_GZ, CZ) + trailing)
    shaped = shaped.transpose((2, 0, 4, 1, 3, 5) + tuple(range(6, 6 + len(trailing))))
    return shaped.reshape((N_GY, N_GX * N_GZ * CX * CY * CZ) + trailing)

def reference(distribution, block_ids, cell_counts, owner, restitution):
    slot_index = jnp.arange(MAXB, dtype=jnp.int32)
    live = slot_index < cell_counts[..., None]
    listed = jnp.where(live, block_ids, -1)

    def plane_step(plane_index):
        prev_plane = (plane_index + NX - 1) % NX
        next_plane = (plane_index + 1) % NX
        values = distribution[plane_index]
        own_ids = listed[plane_index]
        neighbours = [(distribution[prev_plane], listed[prev_plane], distribution[next_plane], listed[next_plane]), (jnp.roll(values, 1, 0), jnp.roll(own_ids, 1, 0), jnp.roll(values, -1, 0), jnp.roll(own_ids, -1, 0)), (jnp.roll(values, 1, 1), jnp.roll(own_ids, 1, 1), jnp.roll(values, -1, 1), jnp.roll(own_ids, -1, 1))]
        live_mask = live[plane_index].astype(jnp.float32)
        read = transport(values, block_ids[plane_index], own_ids, live_mask, neighbours)
        return relax(read, block_ids[plane_index], live_mask, restitution[plane_index])
    relaxed_cells = lax.map(plane_step, jnp.arange(NX, dtype=jnp.int32))
    owner_rows = to_groups(owner)
    ordering = jnp.argsort(owner_rows, axis=1, stable=True).astype(jnp.int32)
    moved_distribution = jnp.take_along_axis(to_groups(relaxed_cells), ordering[..., None, None], axis=1)
    moved_ids = jnp.take_along_axis(to_groups(block_ids), ordering[..., None], axis=1)
    moved_counts = jnp.take_along_axis(to_groups(cell_counts), ordering, axis=1)
    return (moved_distribution, moved_ids, moved_counts)
```

```python
import math

import jax
import jax.numpy as jnp
import numpy as np
from jax import lax
from jax.experimental import pallas as pl
from jax.experimental.pallas import tpu as pltpu
from jax.sharding import PartitionSpec as P

NV1 = 48
BLK = 8
MAXB = 12
EDGE = NV1 // BLK
VB = BLK**3
TILES = 16
ROWS = MAXB * 8
LANES = 128
STEP_COEFF = 0.6
IMPACT_KIND = 0.02
LAM = STEP_COEFF / (NV1 - 1)
F32 = jnp.float32
BF16 = jnp.bfloat16


def iota(shape, dim):
    return lax.broadcasted_iota(jnp.int32, shape, dim)


def mm(a, b):
    return jnp.dot(a.astype(BF16), b.astype(BF16), preferred_element_type=F32)


def spread(rows):
    pick = (iota((8, LANES), 1) % 8 == iota((8, LANES), 0)).astype(F32)
    return mm(rows.astype(F32), pick)


def listed_rows(ids_ref, cnt_ref):
    slots = (iota((MAXB, LANES), 1) // 8 == iota((MAXB, LANES), 0)).astype(F32)
    wide = mm(ids_ref[...].astype(F32), slots)
    mine = iota((LANES, LANES), 1) % 8 == iota((LANES, LANES), 0) % 8
    ids = jnp.sum(jnp.where(mine, wide, 0.0).reshape(TILES, 8, LANES), axis=1)
    lane = iota((TILES, LANES), 1)
    live = ((lane // 8).astype(F32) < spread(cnt_ref[...])) & (lane < ROWS)
    return ids, live


def halo_kernel(d_ref, ids_ref, cnt_ref, ylo, yhi, zlo, zhi, xlo, xhi):
    ids, live = listed_rows(ids_ref, cnt_ref)
    listed = jnp.where(live, ids, -1.0)
    xlo[...] = listed[:8]
    xhi[...] = listed[8:]
    for out, y in ((ylo, 0), (yhi, 7)):
        for x in range(2):
            out[x, :ROWS, :] = d_ref[x * 8 + y]
            row = jnp.broadcast_to(listed[x * 8 + y : x * 8 + y + 1], (8, LANES))
            tail = jnp.concatenate([row, jnp.zeros((8, VB - LANES), F32)], axis=1)
            out[x, ROWS:, :] = tail.astype(BF16)
    lane = iota((TILES, LANES), 1)
    keys = []
    for z, first in ((0, 112), (7, 96)):
        source = iota((LANES, LANES), 0)
        target = iota((LANES, LANES), 1) - first
        move = ((source == target * 8 + z) & (target >= 0) & (target < MAXB)).astype(F32)
        keys.append(jnp.where((lane >= first) & (lane < first + MAXB), mm(listed, move), -1.0))
    row = iota((32, ROWS), 0)
    wanted = jnp.where(row < 16, row * 8, (row - 16) * 8 + 7)
    valid = (row % 16) < MAXB
    select = ((iota((32, ROWS), 1) == wanted) & valid).astype(BF16)
    key_row = iota((16, LANES), 0) == MAXB
    for i in range(TILES):
        faces = jnp.dot(select, d_ref[i], preferred_element_type=F32)
        for out, start, key in ((zlo, 0, keys[0]), (zhi, 16, keys[1])):
            face = faces[start : start + 16]
            first = jnp.where(key_row, jnp.broadcast_to(key[i : i + 1], (16, LANES)), face[:, :LANES])
            out[i, :, :LANES] = first.astype(BF16)
            out[i, :, LANES:] = face[:, LANES:].astype(BF16)


def local_kernel(d_ref, ylo, yhi, zlo, zhi, ids_ref, cnt_ref, rest_ref, vel_ref, acc_ref, cols_ref):
    ids, live = listed_rows(ids_ref, cnt_ref)
    lane = iota((TILES, LANES), 1)
    tile = iota((TILES, LANES), 0)
    zl = lane % 8
    number = ids.astype(jnp.int32)
    bx, by, bz = number // (EDGE * EDGE), number // EDGE % EDGE, number % EDGE
    half = EDGE // 2
    key = ids * 8.0 + zl.astype(F32)
    none = jnp.full((TILES, LANES), -1.0, F32)
    x_low = tile < 8
    inner = live & ((x_low & (bx < half)) | (jnp.logical_not(x_low) & (bx >= half)))
    z_up = bz >= half
    z_step = jnp.where(z_up, -1.0, 1.0)
    z_edge = (z_up & (zl == 0)) | (jnp.logical_not(z_up) & (zl == 7))
    kz = jnp.where(z_edge, ids + jnp.where(z_up, 4096.0, 8192.0), key + z_step)
    centre = lambda b: b.astype(F32) * BLK + ((BLK - 1) / 2.0 - (NV1 - 1) / 2.0)
    widen = 1.0 + spread(rest_ref[...])
    first = jnp.concatenate(
        [
            jnp.where(inner, key, none),
            jnp.where(live & (by >= half), key, none),
            jnp.where(live & (by < half), key, none),
            jnp.where(live, kz, none),
            centre(bx),
            centre(by),
            centre(bz),
            live.astype(F32),
        ],
        axis=0,
    )
    second = jnp.concatenate(
        [jnp.where(live & jnp.logical_not(inner), key, none), widen * widen / 4.0]
        + [jnp.zeros((TILES, LANES), F32)] * 6,
        axis=0,
    )
    first, second = first.T, second.T
    cols_ref[0] = first
    cols_ref[1] = second
    near = jnp.where(live, key, -2.0)
    zrow = zl[:1].astype(F32)
    one_lane = lane[:1]
    column = lambda which, i: first[:ROWS, which * TILES + i : which * TILES + i + 1]

    def halo_key(ref, x):
        got = ref[x, ROWS:, :LANES].astype(F32)[:1]
        return jnp.where(got < 0.0, -2.0, got * 8.0 + zrow)

    def match(col, row):
        return (col == row).astype(F32).astype(BF16)

    for i in range(TILES):
        x, y = divmod(i, 8)
        own = d_ref[i]
        f = own.astype(F32)
        other = (1 - x) * 8 + y
        gx = jnp.dot(match(column(0, i), near[other : other + 1, :ROWS]), d_ref[other], preferred_element_type=F32)
        low, low_key = (ylo[x, :ROWS, :], halo_key(ylo, x)) if y == 0 else (d_ref[i - 1], near[i - 1 : i])
        high, high_key = (yhi[x, :ROWS, :], halo_key(yhi, x)) if y == 7 else (d_ref[i + 1], near[i + 1 : i + 2])
        gy = jnp.dot(match(column(1, i), low_key[:, :ROWS]), low, preferred_element_type=F32)
        gy = gy + jnp.dot(match(column(2, i), high_key[:, :ROWS]), high, preferred_element_type=F32)
        edge = jnp.maximum(zlo[i, :, :LANES].astype(F32)[MAXB : MAXB + 1], zhi[i, :, :LANES].astype(F32)[MAXB : MAXB + 1])
        edge = jnp.where(edge < 0.0, -2.0, edge + jnp.where(one_lane < 112, 4096.0, 8192.0))
        zkey = jnp.where(one_lane < ROWS, near[i : i + 1], edge)
        around = jnp.concatenate([own, zlo[i], zhi[i]], axis=0)
        gz = jnp.dot(match(column(3, i), zkey), around, preferred_element_type=F32)
        acc = f
        for d, g in enumerate((gx, gy, gz)):
            speed = jnp.abs(LAM * column(4 + d, i) + vel_ref[3 + d : 4 + d])
            acc = acc + speed * (g - f)
        acc_ref[i] = acc * column(7, i)


def route_kernel(ids_ref, cnt_ref, own_ref, sel_ref, meta_ref):
    lane = iota((TILES, LANES), 1)
    here = lane // 8 == iota((TILES, LANES), 0)
    flat = lambda v: jnp.sum(jnp.where(here, spread(v), 0.0), axis=0, keepdims=True)
    owner, count = flat(own_ref[...]), flat(cnt_ref[...])
    sub = iota((LANES, LANES), 0)
    cols = jnp.where(sub == 0, owner, jnp.where(sub == 1, count, 0.0)).T
    earlier = (cols[:, :1] == owner) & (sub < iota((LANES, LANES), 1))
    rank = jnp.sum(earlier.astype(F32), axis=0, keepdims=True)
    target = jnp.concatenate([owner * 8.0 + rank + 2.0 * s for s in range(4)], axis=1)
    sel_ref[...] = (iota((512, 512), 0).astype(F32) == target).astype(F32).astype(BF16)
    place = (sub.astype(F32) == owner * 2.0 + rank).astype(F32)
    wide = mm(ids_ref[...].astype(F32), (iota((MAXB, LANES), 0) == iota((MAXB, LANES), 1)).astype(F32))
    info = jnp.where(iota((LANES, LANES), 1) == MAXB, cols[:, 1:2], wide)
    meta_ref[...] = mm(place, info).astype(BF16)


def final_kernel(acc_ref, lo_ref, hi_ref, lokey, hikey, cols_ref, vel_ref, wts_ref, sel_ref, out_ref, read, rows):
    first, second = cols_ref[0], cols_ref[1]
    zrow = (iota((8, LANES), 1) % 8).astype(F32)
    keys = []
    for ref in (lokey, hikey):
        got = ref[...]
        keys.append(jnp.where(got < 0.0, -2.0, got * 8.0 + zrow))
    lane = iota((1, LANES), 1)
    pick = lambda *pairs: sum((lane == at).astype(F32) * value for at, value in pairs)
    plain = pick((0, 1.0), (4, 1.0), (5, 1.0), (6, 1.0), (11, 1.0))
    linear = [pick((1 + d, 1.0), (8 + d, 2.0)) for d in range(3)]
    square = pick((7, 1.0))
    column = lambda src, which, i: src[:ROWS, which * TILES + i : which * TILES + i + 1]
    totals = []
    for i in range(TILES):
        x, y = divmod(i, 8)
        key = keys[x][y : y + 1, :ROWS]
        pick_rows = (column(second, 0, i) == key).astype(F32).astype(BF16)
        g = jnp.dot(pick_rows, (lo_ref, hi_ref)[x][y], preferred_element_type=F32)
        c = [column(first, 4 + d, i) for d in range(3)]
        speed = jnp.abs(LAM * c[0] + vel_ref[3:4])
        now = (acc_ref[i] + speed * g).astype(BF16)
        read[i] = now
        sums = jnp.dot(now, wts_ref[...], preferred_element_type=F32)
        norm = c[0] * c[0] + c[1] * c[1] + c[2] * c[2]
        factor = plain + c[0] * linear[0] + c[1] * linear[1] + c[2] * linear[2] + norm * square
        totals.append(jnp.sum((sums * factor).reshape(MAXB, 8, LANES), axis=0))
    total = jnp.concatenate(totals, axis=0)
    at = lambda k: total[:, k : k + 1]
    mass = at(0)
    u = [(at(1 + d) + at(4 + d)) / mass for d in range(3)]
    energy = at(7) + at(8) + at(9) + at(10) + at(11)
    warm = (energy / mass - (u[0] * u[0] + u[1] * u[1] + u[2] * u[2])) / 3.0
    widen = jnp.concatenate([column(second, 1, i)[:8] for i in range(TILES)], axis=0)
    aim = warm * widen
    rate = 1.0 - jnp.exp(-IMPACT_KIND * (mass / VB) * jnp.sqrt(warm))
    spread_ = 2.0 * math.pi * aim
    scale = mass / (spread_ * jnp.sqrt(spread_))
    sharp = -0.5 * math.log2(math.e) / aim
    for i in range(TILES):
        cell = lambda v: jnp.concatenate([v[i * 8 : i * 8 + 8]] * MAXB, axis=0)
        now = read[i].astype(F32)
        dist = None
        for d in range(3):
            off = (column(first, 4 + d, i) - cell(u[d])) + vel_ref[d : d + 1]
            dist = off * off if dist is None else dist + off * off
        bell = cell(scale) * jnp.exp2(cell(sharp) * dist)
        after = now + (cell(rate) * column(first, 7, i)) * (bell - now)
        rows[:, i * 8 : i * 8 + 8, :] = after.reshape(MAXB, 8, VB).astype(BF16)
    for t in range(3):
        part = rows[4 * t : 4 * t + 4].reshape(512, VB)
        out = jnp.dot(sel_ref[...], part, preferred_element_type=F32)
        out_ref[:, 8 * t : 8 * t + 8, :] = out.reshape(64, 8, VB).astype(BF16)


def unpack_kernel(got_ref, meta_ref, out_ref, ids_ref, cnt_ref):
    row, col = iota((256, 256), 0), iota((256, 256), 1)
    source = (row % 64) // 2 * 8 + row // 64 * 2 + row % 2
    perm = (col == source).astype(F32).astype(BF16)
    for t in range(3):
        for g in range(2):
            part = got_ref[32 * g : 32 * g + 32, 8 * t : 8 * t + 8, :].reshape(256, VB)
            out = jnp.dot(perm, part, preferred_element_type=F32)
            out_ref[4 * t : 4 * t + 4, 64 * g : 64 * g + 64, :] = out.reshape(4, 64, VB).astype(BF16)
    info = meta_ref[...].astype(F32).T.astype(jnp.int32)
    ids_ref[...] = info[:MAXB]
    cnt_ref[...] = info[MAXB : MAXB + 1]


def call(kernel, outs, name, scratch=(), flops=0, moved=0):
    return pl.pallas_call(
        kernel,
        out_shape=[jax.ShapeDtypeStruct(s, d) for s, d in outs],
        scratch_shapes=list(scratch),
        compiler_params=pltpu.CompilerParams(vmem_limit_bytes=48 << 20),
        cost_estimate=pl.CostEstimate(flops=flops, bytes_accessed=moved, transcendentals=0),
        name=name,
    )


def tables():
    j = np.arange(VB)
    w = np.stack([j // (BLK * BLK), j // BLK % BLK, j % BLK]).astype(np.float32) - (BLK - 1) / 2.0
    vel = np.zeros((8, VB), np.float32)
    vel[:3] = w
    vel[3:6] = np.float32(LAM) * w
    weights = np.zeros((VB, LANES), np.float32)
    weights[:, [0, 1, 2, 3, 7]] = 1.0
    for d in range(3):
        weights[:, 4 + d] = w[d]
        weights[:, 8 + d] = w[d]
    weights[:, 11] = (w * w).sum(0)
    return vel, weights


def on_device(distribution, block_ids, cell_counts, owner, restitution):
    nx, ny, nz = (lax.axis_size(a) for a in ("gx", "gy", "gz"))

    def up(v, axis, n):
        return lax.ppermute(v, axis, [(i, (i + 1) % n) for i in range(n)])

    def down(v, axis, n):
        return lax.ppermute(v, axis, [((i + 1) % n, i) for i in range(n)])

    d = distribution.transpose(0, 1, 3, 2, 4).reshape(TILES, ROWS, VB)
    ids = block_ids.reshape(TILES * 8, MAXB)
    cnt = cell_counts.reshape(TILES, 8)
    own = owner.reshape(TILES, 8)
    rest = restitution.reshape(TILES, 8)
    vel, weights = tables()
    vel, weights = jnp.asarray(vel), jnp.asarray(weights, BF16)

    x_hi = down(d[:8], "gx", nx)
    x_lo = up(d[8:], "gx", nx)
    face_y, face_z = ((2, ROWS + 8, VB), BF16), ((TILES, 16, VB), BF16)
    ylo, yhi, zlo, zhi, klo, khi = call(
        halo_kernel, [face_y, face_y, face_z, face_z, ((8, LANES), F32), ((8, LANES), F32)], "halo", flops=10**8, moved=4 * 10**6
    )(d, ids, cnt)
    y_hi, y_lo = down(ylo, "gy", ny), up(yhi, "gy", ny)
    z_hi, z_lo = down(zlo, "gz", nz), up(zhi, "gz", nz)
    k_hi, k_lo = down(klo, "gx", nx), up(khi, "gx", nx)
    acc, cols = call(
        local_kernel, [((TILES, ROWS, VB), F32), ((2, LANES, LANES), F32)], "local", flops=10**9, moved=6 * 10**6
    )(d, y_lo, y_hi, z_lo, z_hi, ids, cnt, rest, vel)
    sel, meta = call(route_kernel, [((512, 512), BF16), ((LANES, LANES), BF16)], "route", flops=10**7, moved=10**6)(ids, cnt, own)
    (out,) = call(
        final_kernel,
        [((64, 24, VB), BF16)],
        "final",
        scratch=[pltpu.VMEM((TILES, ROWS, VB), BF16), pltpu.VMEM((MAXB, LANES, VB), BF16)],
        flops=2 * 10**9,
        moved=8 * 10**6,
    )(acc, x_lo, x_hi, k_lo, k_hi, cols, vel, weights, sel)
    exchange = lambda v: lax.all_to_all(v, ("gx", "gz"), split_axis=0, concat_axis=0, tiled=True)
    got = exchange(out)
    got_meta = exchange(meta.reshape(64, 2, LANES)).reshape(LANES, LANES)
    moved, moved_ids, moved_counts = call(
        unpack_kernel,
        [((MAXB, LANES, VB), BF16), ((MAXB, LANES), jnp.int32), ((1, LANES), jnp.int32)],
        "unpack",
        flops=4 * 10**8,
        moved=4 * 10**6,
    )(got, got_meta)
    return (
        moved.transpose(1, 0, 2).reshape(1, LANES, MAXB, VB),
        moved_ids.T.reshape(1, LANES, MAXB),
        moved_counts,
    )


def solution(mesh):
    placed = (
        P("gx", "gy", "gz", None, None),
        P("gx", "gy", "gz", None),
        P("gx", "gy", "gz"),
        P("gx", "gy", "gz"),
        P("gx", "gy", "gz"),
    )
    return jax.shard_map(
        on_device,
        mesh=mesh,
        in_specs=placed,
        out_specs=(
            P("gy", ("gx", "gz"), None, None),
            P("gy", ("gx", "gz"), None),
            P("gy", ("gx", "gz")),
        ),
        check_vma=False,
    )
```

```python
import functools
import math

import jax
import jax.numpy as jnp
import numpy as np
from jax import lax
from jax.experimental import pallas as pl
from jax.experimental.pallas import tpu as pltpu
from jax.sharding import PartitionSpec as P


NV1 = 48
BLK = 8
MAXB = 12
EDGE = NV1 // BLK
VB = BLK**3
TILES = 16
HALF = 4
ROWS = MAXB * 8
LANES = 128
STEP_COEFF = 0.6
IMPACT_KIND = 0.02
FAR = 1.0e6
LAM = STEP_COEFF / (NV1 - 1)
F32 = jnp.float32
BF16 = jnp.bfloat16


def iota(shape, dim):
    return lax.broadcasted_iota(jnp.int32, shape, dim)


def mm(a, b):
    return jnp.dot(a.astype(BF16), b.astype(BF16), preferred_element_type=F32)


def spread(rows):
    pick = (iota((8, LANES), 1) % 8 == iota((8, LANES), 0)).astype(F32)
    return mm(rows.astype(F32), pick)


def centre(b):
    return b.astype(F32) * BLK + ((BLK - 1) / 2.0 - (NV1 - 1) / 2.0)


def listed_rows(ids_ref, cnt_ref):
    slots = (iota((MAXB, LANES), 1) // 8 == iota((MAXB, LANES), 0)).astype(F32)
    wide = mm(ids_ref[...].astype(F32), slots)
    mine = iota((LANES, LANES), 1) % 8 == iota((LANES, LANES), 0) % 8
    ids = jnp.sum(jnp.where(mine, wide, 0.0).reshape(TILES, 8, LANES), axis=1)
    lane = iota((TILES, LANES), 1)
    live = ((lane // 8).astype(F32) < spread(cnt_ref[...])) & (lane < ROWS)
    return ids, live


def x_copies(part, d_ref, outs, sems):
    copies = []
    for k, out in enumerate(outs):
        source = d_ref.at[pl.ds((8 * k + HALF * part) * ROWS, HALF * ROWS)]
        copies.append(pltpu.make_async_copy(source, out.at[pl.ds(0, HALF * ROWS)], sems.at[k]))
    return copies


def put_keys(listed, outs):
    for k, out in enumerate(outs):
        out[HALF * ROWS :, :LANES] = listed[8 * k : 8 * k + 8].astype(BF16)
        out[HALF * ROWS :, LANES:] = jnp.zeros((8, VB - LANES), BF16)


def face_kernel(d_ref, ids_ref, cnt_ref, lo, hi, sems):
    copies = x_copies(1, d_ref, (lo, hi), sems)
    for copy in copies:
        copy.start()
    ids, live = listed_rows(ids_ref, cnt_ref)
    put_keys(jnp.where(live, ids, -1.0), (lo, hi))
    for copy in copies:
        copy.wait()


def front_kernel(d_hbm, ids_hbm, cnt_hbm, lo, hi, ylo, yhi, zlo, zhi, d_ref, ids_ref, cnt_ref, sems):
    small = [pltpu.make_async_copy(ids_hbm, ids_ref, sems.at[2]), pltpu.make_async_copy(cnt_hbm, cnt_ref, sems.at[3])]
    large = x_copies(0, d_hbm, (lo, hi), sems)
    quarter = TILES // 4 * ROWS
    parts = [pl.ds(q * quarter, quarter) for q in range(4)]
    whole = [pltpu.make_async_copy(d_hbm.at[p], d_ref.at[p], sems.at[4 + q]) for q, p in enumerate(parts)]
    for copy in small + whole + large:
        copy.start()
    for copy in small:
        copy.wait()
    ids, live = listed_rows(ids_ref, cnt_ref)
    listed = jnp.where(live, ids, -1.0)
    put_keys(listed, (lo, hi))
    lane = iota((TILES, LANES), 1)
    keys = []
    for z, first in ((0, 112), (7, 96)):
        source = iota((LANES, LANES), 0)
        target = iota((LANES, LANES), 1) - first
        move = ((source == target * 8 + z) & (target >= 0) & (target < MAXB)).astype(F32)
        keys.append(jnp.where((lane >= first) & (lane < first + MAXB), mm(listed, move), -1.0))
    row = iota((32, ROWS), 0)
    wanted = jnp.where(row < 16, row * 8, (row - 16) * 8 + 7)
    valid = (row % 16) < MAXB
    select = ((iota((32, ROWS), 1) == wanted) & valid).astype(BF16)
    key_row = iota((16, LANES), 0) == MAXB
    for i in range(TILES):
        if i % 4 == 0:
            whole[i // 4].wait()
        tile = d_ref[i * ROWS : i * ROWS + ROWS, :]
        if i % 8 in (0, 7):
            out = yhi if i % 8 else ylo
            out[i // 8, :ROWS, :] = tile
            tail = jnp.concatenate([jnp.broadcast_to(listed[i : i + 1], (8, LANES)), jnp.zeros((8, VB - LANES), F32)], axis=1)
            out[i // 8, ROWS:, :] = tail.astype(BF16)
        faces = jnp.dot(select, tile, preferred_element_type=F32)
        for out, start, key in ((zlo, 0, keys[0]), (zhi, 16, keys[1])):
            face = faces[start : start + 16]
            first = jnp.where(key_row, jnp.broadcast_to(key[i : i + 1], (16, LANES)), face[:, :LANES])
            out[i, :, :LANES] = first.astype(BF16)
            out[i, :, LANES:] = face[:, LANES:].astype(BF16)
    for copy in large:
        copy.wait()


def local_kernel(d_ref, ylo, yhi, zlo, zhi, ids_ref, cnt_ref, vel_ref, acc_ref):
    ids, live = listed_rows(ids_ref, cnt_ref)
    lane = iota((TILES, LANES), 1)
    tile = iota((TILES, LANES), 0)
    zl = lane % 8
    number = ids.astype(jnp.int32)
    bx, by, bz = number // (EDGE * EDGE), number // EDGE % EDGE, number % EDGE
    half = EDGE // 2
    key = ids * 8.0 + zl.astype(F32)
    none = jnp.full((TILES, LANES), -1.0, F32)
    x_low = tile < 8
    inner = live & ((x_low & (bx < half)) | (jnp.logical_not(x_low) & (bx >= half)))
    z_up = bz >= half
    z_step = jnp.where(z_up, -1.0, 1.0)
    z_edge = (z_up & (zl == 0)) | (jnp.logical_not(z_up) & (zl == 7))
    kz = jnp.where(z_edge, ids + jnp.where(z_up, 4096.0, 8192.0), key + z_step)
    first = jnp.concatenate(
        [
            jnp.where(inner, key, none),
            jnp.where(live & (by >= half), key, none),
            jnp.where(live & (by < half), key, none),
            jnp.where(live, kz, none),
            centre(bx),
            centre(by),
            centre(bz),
            live.astype(F32),
        ],
        axis=0,
    )
    first = first.T
    near = jnp.where(live, key, -2.0)
    zrow = zl[:1].astype(F32)
    one_lane = lane[:1]
    column = lambda which, i: first[:ROWS, which * TILES + i : which * TILES + i + 1]

    def halo_key(ref, x):
        got = ref[x, ROWS:, :LANES].astype(F32)[:1]
        return jnp.where(got < 0.0, -2.0, got * 8.0 + zrow)

    def match(col, row):
        return (col == row).astype(F32).astype(BF16)

    for i in range(TILES):
        x, y = divmod(i, 8)
        own = d_ref[i]
        f = own.astype(F32)
        other = (1 - x) * 8 + y
        gx = jnp.dot(match(column(0, i), near[other : other + 1, :ROWS]), d_ref[other], preferred_element_type=F32)
        low, low_key = (ylo[x, :ROWS, :], halo_key(ylo, x)) if y == 0 else (d_ref[i - 1], near[i - 1 : i])
        high, high_key = (yhi[x, :ROWS, :], halo_key(yhi, x)) if y == 7 else (d_ref[i + 1], near[i + 1 : i + 2])
        gy = jnp.dot(match(column(1, i), low_key[:, :ROWS]), low, preferred_element_type=F32)
        gy = gy + jnp.dot(match(column(2, i), high_key[:, :ROWS]), high, preferred_element_type=F32)
        edge = jnp.maximum(zlo[i, :, :LANES].astype(F32)[MAXB : MAXB + 1], zhi[i, :, :LANES].astype(F32)[MAXB : MAXB + 1])
        edge = jnp.where(edge < 0.0, -2.0, edge + jnp.where(one_lane < 112, 4096.0, 8192.0))
        zkey = jnp.where(one_lane < ROWS, near[i : i + 1], edge)
        around = jnp.concatenate([own, zlo[i], zhi[i]], axis=0)
        gz = jnp.dot(match(column(3, i), zkey), around, preferred_element_type=F32)
        acc = f
        for d, g in enumerate((gx, gy, gz)):
            speed = jnp.abs(LAM * column(4 + d, i) + vel_ref[3 + d : 4 + d])
            acc = acc + speed * (g - f)
        acc_ref[i] = acc * column(7, i)


def route_kernel(ids_ref, cnt_ref, own_ref, rest_ref, sel_ref, meta_ref, key_ref, cen_ref, fac_ref, widen_ref):
    lane = iota((TILES, LANES), 1)
    here = lane // 8 == iota((TILES, LANES), 0)
    flat = lambda v: jnp.sum(jnp.where(here, spread(v), 0.0), axis=0, keepdims=True)
    owner, count = flat(own_ref[...]), flat(cnt_ref[...])
    sub = iota((LANES, LANES), 0)
    cols = jnp.where(sub == 0, owner, jnp.where(sub == 1, count, 0.0)).T
    earlier = (cols[:, :1] == owner) & (sub < iota((LANES, LANES), 1))
    rank = jnp.sum(earlier.astype(F32), axis=0, keepdims=True)
    home = owner * 8.0 + rank
    for part in range(2):
        mine = jnp.concatenate([home[:, 64 * x + 32 * part : 64 * x + 32 * part + 32] for x in range(2)], axis=1)
        target = jnp.concatenate([mine + 2.0 * s for s in range(4)], axis=1)
        sel_ref[part] = (iota((512, 256), 0).astype(F32) == target).astype(F32).astype(BF16)
    place = (iota((512, LANES), 0).astype(F32) == home).astype(F32)
    wide = mm(ids_ref[...].astype(F32), (iota((MAXB, LANES), 0) == iota((MAXB, LANES), 1)).astype(F32))
    info = jnp.where(iota((LANES, LANES), 1) == MAXB, cols[:, 1:2], wide)
    meta_ref[...] = mm(place, info).astype(BF16)

    ids, live = listed_rows(ids_ref, cnt_ref)
    number = ids.astype(jnp.int32)
    bx, by, bz = number // (EDGE * EDGE), number // EDGE % EDGE, number % EDGE
    outer = live & (((iota((TILES, LANES), 0) < 8) & (bx >= EDGE // 2)) | ((iota((TILES, LANES), 0) >= 8) & (bx < EDGE // 2)))
    widen = 1.0 + spread(rest_ref[...])
    table = jnp.concatenate(
        [
            jnp.where(outer, ids * 8.0 + (lane % 8).astype(F32), -1.0),
            centre(bx),
            centre(by),
            centre(bz),
            live.astype(F32),
            widen * widen / 4.0,
            jnp.zeros((2 * TILES, LANES), F32),
        ],
        axis=0,
    ).T
    one = iota((1, LANES), 1)
    pick = lambda *pairs: sum((one == at).astype(F32) * value for at, value in pairs)
    plain = pick((0, 1.0), (4, 1.0), (5, 1.0), (6, 1.0), (11, 1.0))
    linear = [pick((1 + d, 1.0), (8 + d, 2.0)) for d in range(3)]
    square = pick((7, 1.0))
    for i in range(TILES):
        wide = lambda which: jnp.broadcast_to(table[:ROWS, which * TILES + i : which * TILES + i + 1], (ROWS, LANES))
        key_ref[i] = wide(0)
        c = [wide(1 + d) for d in range(3)]
        norm = c[0] * c[0] + c[1] * c[1] + c[2] * c[2]
        fac_ref[i] = plain + c[0] * linear[0] + c[1] * linear[1] + c[2] * linear[2] + norm * square
        cen_ref[0, i] = c[0]
        cen_ref[1, i] = jnp.where(wide(4) > 0.0, c[1], FAR)
        cen_ref[2, i] = c[2]
        widen_ref[i] = wide(5)[:8]


def final_kernel(
    part, acc_ref, lo_ref, hi_ref, key_ref, cen_ref, fac_ref, widen_ref, vel_ref, wts_ref, sel_ref, prev_ref, out_ref,
    read, rows, total_ref, cell_ref,
):
    zrow = (iota((8, LANES), 1) % 8).astype(F32)
    tiles4 = [slice(LANES * t, LANES * t + LANES) for t in range(4)]
    places = [(x, y, x * 8 + HALF * part + y, x * HALF + y) for y in range(HALF) for x in range(2)]
    slots = lambda v: v.reshape(MAXB, 8, LANES)
    near = []
    for ref in (lo_ref, hi_ref):
        got = ref[HALF * ROWS :, :LANES].astype(F32)
        near.append(jnp.where(got < 0.0, -2.0, got * 8.0 + zrow))

    for x, y, i, k in places:
        halo = (lo_ref, hi_ref)[x][y * ROWS : y * ROWS + ROWS, :]
        row = near[x][HALF * part + y : HALF * part + y + 1]
        pick_rows = (key_ref[i][:, :ROWS] == row[:, :ROWS]).astype(F32).astype(BF16)
        g = jnp.dot(pick_rows, halo, preferred_element_type=F32)
        cx = cen_ref[0, i]
        speed = jnp.abs(LAM * cx + vel_ref[3:4, :LANES])
        step = jnp.where(cx > 0.0, 2.0 * LAM, -2.0 * LAM)
        parts = []
        for at in tiles4:
            parts.append((acc_ref[i, :, at] + speed * g[:, at]).astype(BF16))
            speed = speed + step
        now = jnp.concatenate(parts, axis=1)
        read[k] = now
        sums = jnp.dot(now, wts_ref[...], preferred_element_type=F32)
        total_ref[k] = jnp.sum(slots(sums * fac_ref[i]), axis=0)

    cells = 2 * HALF * 8
    total = total_ref[...].reshape(cells, LANES)
    at = lambda k: total[:, k : k + 1]
    mass = at(0)
    per = 1.0 / mass
    u = [(at(1 + d) + at(4 + d)) * per for d in range(3)]
    energy = at(7) + at(8) + at(9) + at(10) + at(11)
    warm = (energy * per - (u[0] * u[0] + u[1] * u[1] + u[2] * u[2])) / 3.0
    widen = jnp.concatenate([widen_ref[x * 8 + HALF * part : x * 8 + HALF * part + HALF] for x in range(2)], axis=0)
    aim = warm * widen.reshape(cells, LANES)[:, :1]
    rate = 1.0 - jnp.exp(-IMPACT_KIND * (mass / VB) * jnp.sqrt(warm))
    area = 2.0 * math.pi * aim
    scale = rate * mass / (area * jnp.sqrt(area))
    sharp = 0.5 * math.log2(math.e) / aim
    for k, v in enumerate((u[0], u[1], u[2], -sharp, jnp.sqrt(sharp), scale, 1.0 - rate)):
        cell_ref[k] = jnp.broadcast_to(v, (cells, LANES)).reshape(2 * HALF, 8, LANES)

    for x, y, i, k in places:
        ux, uy, uz, fall, root, scale, keep = (cell_ref[q, k][None] for q in range(7))
        off_y = slots(cen_ref[1, i]) - uy + vel_ref[1:2, :LANES][None]
        off_z = slots(cen_ref[2, i]) - uz + vel_ref[2:3, :LANES][None]
        side = (off_y * off_y + off_z * off_z) * fall
        off_x = (slots(cen_ref[0, i]) - ux + vel_ref[:1, :LANES][None]) * root
        step = root + root
        for at in tiles4:
            now = slots(read[k, :, at].astype(F32))
            after = now * keep + scale * jnp.exp2(side - off_x * off_x)
            rows[:, k * 8 : k * 8 + 8, at] = after.astype(BF16)
            off_x = off_x + step

    for t in range(3):
        out = jnp.dot(sel_ref[part], rows[4 * t : 4 * t + 4].reshape(256, VB), preferred_element_type=F32)
        for k, at in enumerate(tiles4):
            where = slice(32 * t + 8 * k, 32 * t + 8 * k + 8)
            block = out[:, at].reshape(64, 8, LANES)
            if part:
                block = block + prev_ref[:, where, :].astype(F32)
            out_ref[:, where, :] = block.astype(BF16)
    out_ref[:, 96:, :] = prev_ref[:, 96:, :] if part else prev_ref[...].reshape(64, 8, LANES)


def unpack_kernel(got_ref, out_ref, ids_ref, cnt_ref, rows, sems):
    row, col = iota((256, 256), 0), iota((256, 256), 1)
    source = (row % 64) // 2 * 8 + row // 64 * 2 + row % 2
    perm = (col == source).astype(F32).astype(BF16)
    place = iota((LANES, 512), 0)
    pick = (iota((LANES, 512), 1) == place // 2 * 8 + place % 2).astype(F32).astype(BF16)
    meta = got_ref[:, 96:, :].reshape(512, LANES)
    info = jnp.dot(pick, meta, preferred_element_type=F32).T.astype(jnp.int32)
    copies = []
    for t in range(3):
        for g in range(2):
            parts = [got_ref[32 * g : 32 * g + 32, 32 * t + 8 * k : 32 * t + 8 * k + 8, :].reshape(256, LANES) for k in range(4)]
            out = jnp.dot(perm, jnp.concatenate(parts, axis=1), preferred_element_type=F32)
            where = (pl.ds(4 * t, 4), pl.ds(64 * g, 64))
            rows[where] = out.reshape(4, 64, VB).astype(BF16)
            copies.append(pltpu.make_async_copy(rows.at[where], out_ref.at[where], sems.at[2 * t + g]))
            copies[-1].start()
    ids_ref[...] = info[:MAXB].reshape(MAXB, 1, LANES)
    cnt_ref[...] = info[MAXB : MAXB + 1]
    for copy in copies:
        copy.wait()


def call(kernel, outs, scratch=(), flops=0, moved=0, vmem=16 << 20, **extra):
    return pl.pallas_call(
        kernel,
        out_shape=[jax.ShapeDtypeStruct(s, d) for s, d in outs],
        scratch_shapes=list(scratch),
        compiler_params=pltpu.CompilerParams(vmem_limit_bytes=vmem),
        cost_estimate=pl.CostEstimate(flops=flops, bytes_accessed=moved, transcendentals=0),
        **extra,
    )


def tables():
    j = np.arange(VB)
    w = np.stack([j // (BLK * BLK), j // BLK % BLK, j % BLK]).astype(np.float32) - (BLK - 1) / 2.0
    vel = np.zeros((8, VB), np.float32)
    vel[:3] = w
    vel[3:6] = np.float32(LAM) * w
    weights = np.zeros((VB, LANES), np.float32)
    weights[:, [0, 1, 2, 3, 7]] = 1.0
    for d in range(3):
        weights[:, 4 + d] = w[d]
        weights[:, 8 + d] = w[d]
    weights[:, 11] = (w * w).sum(0)
    return vel, weights


def advance(distribution, block_ids, cell_counts, owner, restitution):
    nx, ny, nz = (lax.axis_size(a) for a in ("gx", "gy", "gz"))

    def up(v, axis, n):
        return lax.ppermute(v, axis, [(i, (i + 1) % n) for i in range(n)])

    def down(v, axis, n):
        return lax.ppermute(v, axis, [((i + 1) % n, i) for i in range(n)])

    d = distribution.transpose(0, 1, 3, 2, 4).reshape(TILES, ROWS, VB)
    ids = block_ids.reshape(TILES * 8, MAXB)
    cnt = cell_counts.reshape(TILES, 8)
    own = owner.reshape(TILES, 8)
    rest = restitution.reshape(TILES, 8)
    vel, weights = tables()
    vel, weights = jnp.asarray(vel), jnp.asarray(weights, BF16)

    face_x = ((HALF * ROWS + 8, VB), BF16)
    face_y, face_z = ((2, ROWS + 8, VB), BF16), ((TILES, 16, VB), BF16)
    flat = d.reshape(TILES * ROWS, VB)
    hbm, whole = pl.BlockSpec(memory_space=pltpu.HBM), pl.BlockSpec(memory_space=pltpu.VMEM)
    xlo, xhi, ylo, yhi, zlo, zhi = call(
        front_kernel,
        [face_x, face_x, face_y, face_y, face_z, face_z],
        scratch=[
            pltpu.VMEM((TILES * ROWS, VB), BF16),
            pltpu.VMEM((TILES * 8, MAXB), jnp.int32),
            pltpu.VMEM((TILES, 8), jnp.int32),
            pltpu.SemaphoreType.DMA((8,)),
        ],
        flops=10**8,
        moved=4 * 10**6,
        in_specs=[hbm] * 3,
    )(*(pltpu.with_memory_space_constraint(v, pltpu.HBM) for v in (flat, ids, cnt)))
    near_x = [(up(xhi, "gx", nx), down(xlo, "gx", nx))]
    xlo, xhi = call(
        face_kernel,
        [face_x, face_x],
        scratch=[pltpu.SemaphoreType.DMA((2,))],
        moved=2 * 10**6,
        in_specs=[pl.BlockSpec(memory_space=pl.ANY), whole, whole],
    )(flat, ids, cnt)
    near_x.append((up(xhi, "gx", nx), down(xlo, "gx", nx)))
    y_hi, y_lo = down(ylo, "gy", ny), up(yhi, "gy", ny)
    z_hi, z_lo = down(zlo, "gz", nz), up(zhi, "gz", nz)
    (acc,) = call(local_kernel, [((TILES, ROWS, VB), F32)], flops=10**9, moved=6 * 10**6)(
        d, y_lo, y_hi, z_lo, z_hi, ids, cnt, vel
    )
    wide = ((TILES, ROWS, LANES), F32)
    sel, meta, keys, centres, factors, widen = call(
        route_kernel,
        [((2, 512, 256), BF16), ((512, LANES), BF16), wide, ((3, TILES, ROWS, LANES), F32), wide, ((TILES, 8, LANES), F32)],
        flops=10**7,
        moved=10**6,
    )(ids, cnt, own, rest)
    out = meta
    for part in range(2):
        (out,) = call(
            functools.partial(final_kernel, part),
            [((64, 104, LANES), BF16)],
            scratch=[
                pltpu.VMEM((2 * HALF, ROWS, VB), BF16),
                pltpu.VMEM((MAXB, 2 * HALF * 8, VB), BF16),
                pltpu.VMEM((2 * HALF, 8, LANES), F32),
                pltpu.VMEM((7, 2 * HALF, 8, LANES), F32),
            ],
            flops=10**9,
            moved=4 * 10**6,
        )(acc, *near_x[part], keys, centres, factors, widen, vel, weights, sel, out)
    got = lax.all_to_all(out, ("gx", "gz"), split_axis=0, concat_axis=0, tiled=True)
    moved, moved_ids, moved_counts = call(
        unpack_kernel,
        [((MAXB, LANES, VB), BF16), ((MAXB, 1, LANES), jnp.int32), ((1, LANES), jnp.int32)],
        scratch=[pltpu.VMEM((MAXB, LANES, VB), BF16), pltpu.SemaphoreType.DMA((6,))],
        flops=4 * 10**8,
        moved=4 * 10**6,
        out_specs=[pl.BlockSpec(memory_space=pl.ANY), whole, whole],
    )(got)
    return (
        moved.transpose(1, 0, 2).reshape(1, LANES, MAXB, VB),
        moved_ids.transpose(1, 2, 0),
        moved_counts,
    )


def solution(mesh):
    placed = (
        P("gx", "gy", "gz", None, None),
        P("gx", "gy", "gz", None),
        P("gx", "gy", "gz"),
        P("gx", "gy", "gz"),
        P("gx", "gy", "gz"),
    )
    return jax.shard_map(
        advance,
        mesh=mesh,
        in_specs=placed,
        out_specs=(
            P("gy", ("gx", "gz"), None, None),
            P("gy", ("gx", "gz"), None),
            P("gy", ("gx", "gz")),
        ),
        check_vma=False,
    )
```

```python
import functools
import math

import jax
import jax.numpy as jnp
import numpy as np
from jax import lax
from jax.experimental import pallas as pl
from jax.experimental.pallas import tpu as pltpu
from jax.sharding import PartitionSpec as P


NV1 = 48
BLK = 8
MAXB = 12
EDGE = NV1 // BLK
VB = BLK**3
TILES = 16
HALF = 4
ROWS = MAXB * 8
LANES = 128
STEP_COEFF = 0.6
IMPACT_KIND = 0.02
FAR = 1.0e6
LAM = STEP_COEFF / (NV1 - 1)
F32 = jnp.float32
BF16 = jnp.bfloat16


def iota(shape, dim):
    return lax.broadcasted_iota(jnp.int32, shape, dim)


def mm(a, b):
    return jnp.dot(a.astype(BF16), b.astype(BF16), preferred_element_type=F32)


def spread(rows):
    pick = (iota((8, LANES), 1) % 8 == iota((8, LANES), 0)).astype(F32)
    return mm(rows.astype(F32), pick)


def centre(b):
    return b.astype(F32) * BLK + ((BLK - 1) / 2.0 - (NV1 - 1) / 2.0)


def listed_rows(ids_ref, cnt_ref):
    slots = (iota((MAXB, LANES), 1) // 8 == iota((MAXB, LANES), 0)).astype(F32)
    wide = mm(ids_ref[...].astype(F32), slots)
    mine = iota((LANES, LANES), 1) % 8 == iota((LANES, LANES), 0) % 8
    ids = jnp.sum(jnp.where(mine, wide, 0.0).reshape(TILES, 8, LANES), axis=1)
    lane = iota((TILES, LANES), 1)
    live = ((lane // 8).astype(F32) < spread(cnt_ref[...])) & (lane < ROWS)
    return ids, live


def x_copies(part, d_ref, outs, sems):
    copies = []
    for k, out in enumerate(outs):
        source = d_ref.at[pl.ds((8 * k + HALF * part) * ROWS, HALF * ROWS)]
        copies.append(pltpu.make_async_copy(source, out.at[pl.ds(0, HALF * ROWS)], sems.at[k]))
    return copies


def put_keys(listed, outs):
    for k, out in enumerate(outs):
        out[HALF * ROWS :, :LANES] = listed[8 * k : 8 * k + 8].astype(BF16)
        out[HALF * ROWS :, LANES:] = jnp.zeros((8, VB - LANES), BF16)


def face_kernel(d_ref, ids_ref, cnt_ref, lo, hi, sems):
    copies = x_copies(1, d_ref, (lo, hi), sems)
    for copy in copies:
        copy.start()
    ids, live = listed_rows(ids_ref, cnt_ref)
    put_keys(jnp.where(live, ids, -1.0), (lo, hi))
    for copy in copies:
        copy.wait()


def front_kernel(
    d_hbm, ids_hbm, cnt_hbm, own_hbm, rest_hbm, lo, hi, ylo, yhi, zlo, zhi, ids_ref, cnt_ref, own_ref, rest_ref, d_ref, sems
):
    small = [pltpu.make_async_copy(ids_hbm, ids_ref, sems.at[2]), pltpu.make_async_copy(cnt_hbm, cnt_ref, sems.at[3])]
    later = [pltpu.make_async_copy(own_hbm, own_ref, sems.at[8]), pltpu.make_async_copy(rest_hbm, rest_ref, sems.at[9])]
    large = x_copies(0, d_hbm, (lo, hi), sems)
    quarter = TILES // 4 * ROWS
    parts = [pl.ds(q * quarter, quarter) for q in range(4)]
    whole = [pltpu.make_async_copy(d_hbm.at[p], d_ref.at[p], sems.at[4 + q]) for q, p in enumerate(parts)]
    for copy in small + whole + large + later:
        copy.start()
    for copy in small:
        copy.wait()
    ids, live = listed_rows(ids_ref, cnt_ref)
    listed = jnp.where(live, ids, -1.0)
    put_keys(listed, (lo, hi))
    lane = iota((TILES, LANES), 1)
    keys = []
    for z, first in ((0, 112), (7, 96)):
        source = iota((LANES, LANES), 0)
        target = iota((LANES, LANES), 1) - first
        move = ((source == target * 8 + z) & (target >= 0) & (target < MAXB)).astype(F32)
        keys.append(jnp.where((lane >= first) & (lane < first + MAXB), mm(listed, move), -1.0))
    row = iota((32, ROWS), 0)
    wanted = jnp.where(row < 16, row * 8, (row - 16) * 8 + 7)
    valid = (row % 16) < MAXB
    select = ((iota((32, ROWS), 1) == wanted) & valid).astype(BF16)
    key_row = iota((16, LANES), 0) == MAXB
    for i in range(TILES):
        if i % 4 == 0:
            whole[i // 4].wait()
        tile = d_ref[i * ROWS : i * ROWS + ROWS, :]
        if i % 8 in (0, 7):
            out = yhi if i % 8 else ylo
            out[i // 8, :ROWS, :] = tile
            tail = jnp.concatenate([jnp.broadcast_to(listed[i : i + 1], (8, LANES)), jnp.zeros((8, VB - LANES), F32)], axis=1)
            out[i // 8, ROWS:, :] = tail.astype(BF16)
        faces = jnp.dot(select, tile, preferred_element_type=F32)
        for out, start, key in ((zlo, 0, keys[0]), (zhi, 16, keys[1])):
            face = faces[start : start + 16]
            first = jnp.where(key_row, jnp.broadcast_to(key[i : i + 1], (16, LANES)), face[:, :LANES])
            out[i, :, :LANES] = first.astype(BF16)
            out[i, :, LANES:] = face[:, LANES:].astype(BF16)
    for copy in large + later:
        copy.wait()


def local_kernel(d_ref, ylo, yhi, zlo, zhi, ids_ref, cnt_ref, vel_ref, acc_ref):
    ids, live = listed_rows(ids_ref, cnt_ref)
    lane = iota((TILES, LANES), 1)
    tile = iota((TILES, LANES), 0)
    zl = lane % 8
    number = ids.astype(jnp.int32)
    bx, by, bz = number // (EDGE * EDGE), number // EDGE % EDGE, number % EDGE
    half = EDGE // 2
    key = ids * 8.0 + zl.astype(F32)
    none = jnp.full((TILES, LANES), -1.0, F32)
    x_low = tile < 8
    inner = live & ((x_low & (bx < half)) | (jnp.logical_not(x_low) & (bx >= half)))
    z_up = bz >= half
    z_step = jnp.where(z_up, -1.0, 1.0)
    z_edge = (z_up & (zl == 0)) | (jnp.logical_not(z_up) & (zl == 7))
    kz = jnp.where(z_edge, ids + jnp.where(z_up, 4096.0, 8192.0), key + z_step)
    first = jnp.concatenate(
        [
            jnp.where(inner, key, none),
            jnp.where(live & (by >= half), key, none),
            jnp.where(live & (by < half), key, none),
            jnp.where(live, kz, none),
            centre(bx),
            centre(by),
            centre(bz),
            live.astype(F32),
        ],
        axis=0,
    )
    first = first.T
    near = jnp.where(live, key, -2.0)
    zrow = zl[:1].astype(F32)
    one_lane = lane[:1]
    column = lambda which, i: first[:ROWS, which * TILES + i : which * TILES + i + 1]

    def halo_key(ref, x):
        got = ref[x, ROWS:, :LANES].astype(F32)[:1]
        return jnp.where(got < 0.0, -2.0, got * 8.0 + zrow)

    def match(col, row):
        return (col == row).astype(F32).astype(BF16)

    for i in range(TILES):
        x, y = divmod(i, 8)
        own = d_ref[i]
        f = own.astype(F32)
        other = (1 - x) * 8 + y
        gx = jnp.dot(match(column(0, i), near[other : other + 1, :ROWS]), d_ref[other], preferred_element_type=F32)
        low, low_key = (ylo[x, :ROWS, :], halo_key(ylo, x)) if y == 0 else (d_ref[i - 1], near[i - 1 : i])
        high, high_key = (yhi[x, :ROWS, :], halo_key(yhi, x)) if y == 7 else (d_ref[i + 1], near[i + 1 : i + 2])
        gy = jnp.dot(match(column(1, i), low_key[:, :ROWS]), low, preferred_element_type=F32)
        gy = gy + jnp.dot(match(column(2, i), high_key[:, :ROWS]), high, preferred_element_type=F32)
        edge = jnp.maximum(zlo[i, :, :LANES].astype(F32)[MAXB : MAXB + 1], zhi[i, :, :LANES].astype(F32)[MAXB : MAXB + 1])
        edge = jnp.where(edge < 0.0, -2.0, edge + jnp.where(one_lane < 112, 4096.0, 8192.0))
        zkey = jnp.where(one_lane < ROWS, near[i : i + 1], edge)
        around = jnp.concatenate([own, zlo[i], zhi[i]], axis=0)
        gz = jnp.dot(match(column(3, i), zkey), around, preferred_element_type=F32)
        acc = f
        for d, g in enumerate((gx, gy, gz)):
            speed = jnp.abs(LAM * column(4 + d, i) + vel_ref[3 + d : 4 + d])
            acc = acc + speed * (g - f)
        acc_ref[i] = acc * column(7, i)


def route_kernel(ids_ref, cnt_ref, own_ref, rest_ref, sel_ref, meta_ref, key_ref, cen_ref, fac_ref, widen_ref):
    lane = iota((TILES, LANES), 1)
    here = lane // 8 == iota((TILES, LANES), 0)
    flat = lambda v: jnp.sum(jnp.where(here, spread(v), 0.0), axis=0, keepdims=True)
    owner, count = flat(own_ref[...]), flat(cnt_ref[...])
    sub = iota((LANES, LANES), 0)
    cols = jnp.where(sub == 0, owner, jnp.where(sub == 1, count, 0.0)).T
    earlier = (cols[:, :1] == owner) & (sub < iota((LANES, LANES), 1))
    rank = jnp.sum(earlier.astype(F32), axis=0, keepdims=True)
    home = owner * 8.0 + rank
    for part in range(2):
        mine = jnp.concatenate([home[:, 64 * x + 32 * part : 64 * x + 32 * part + 32] for x in range(2)], axis=1)
        mine = mine.astype(jnp.int32)
        shifts = [(mine % 8 + mine // 8 * 2 + 2 * s) % 8 for s in range(4)]
        target = jnp.concatenate([mine // 8 * 8 + shift for shift in shifts], axis=1).astype(F32)
        sel_ref[part] = (iota((512, 256), 0).astype(F32) == target).astype(F32).astype(BF16)
    phase = 2 * (owner.astype(jnp.int32) % 4)
    place = (iota((512, LANES), 0).astype(F32) == home + phase.astype(F32)).astype(F32)
    wide = mm(ids_ref[...].astype(F32), (iota((MAXB, LANES), 0) == iota((MAXB, LANES), 1)).astype(F32))
    info = jnp.where(iota((LANES, LANES), 1) == MAXB, cols[:, 1:2], wide)
    meta_ref[...] = mm(place, info).astype(BF16)

    ids, live = listed_rows(ids_ref, cnt_ref)
    number = ids.astype(jnp.int32)
    bx, by, bz = number // (EDGE * EDGE), number // EDGE % EDGE, number % EDGE
    outer = live & (((iota((TILES, LANES), 0) < 8) & (bx >= EDGE // 2)) | ((iota((TILES, LANES), 0) >= 8) & (bx < EDGE // 2)))
    widen = 1.0 + spread(rest_ref[...])
    table = jnp.concatenate(
        [
            jnp.where(outer, ids * 8.0 + (lane % 8).astype(F32), -1.0),
            centre(bx),
            centre(by),
            centre(bz),
            live.astype(F32),
            widen * widen / 4.0,
            jnp.zeros((2 * TILES, LANES), F32),
        ],
        axis=0,
    ).T
    one = iota((1, LANES), 1)
    pick = lambda *pairs: sum((one == at).astype(F32) * value for at, value in pairs)
    plain = pick((0, 1.0), (4, 1.0), (5, 1.0), (6, 1.0), (11, 1.0))
    linear = [pick((1 + d, 1.0), (8 + d, 2.0)) for d in range(3)]
    square = pick((7, 1.0))
    for i in range(TILES):
        wide = lambda which: jnp.broadcast_to(table[:ROWS, which * TILES + i : which * TILES + i + 1], (ROWS, LANES))
        key_ref[i] = wide(0)
        c = [wide(1 + d) for d in range(3)]
        norm = c[0] * c[0] + c[1] * c[1] + c[2] * c[2]
        fac_ref[i] = plain + c[0] * linear[0] + c[1] * linear[1] + c[2] * linear[2] + norm * square
        cen_ref[0, i] = c[0]
        cen_ref[1, i] = jnp.where(wide(4) > 0.0, c[1], FAR)
        cen_ref[2, i] = c[2]
        widen_ref[i] = wide(5)[:8]


def final_kernel(
    part, acc_ref, lo_ref, hi_ref, key_ref, cen_ref, fac_ref, widen_ref, vel_ref, wts_ref, sel_ref, prev_ref, out_ref,
    read, rows, total_ref, cell_ref,
):
    zrow = (iota((8, LANES), 1) % 8).astype(F32)
    tiles4 = [slice(LANES * t, LANES * t + LANES) for t in range(4)]
    places = [(x, y, x * 8 + HALF * part + y, x * HALF + y) for y in range(HALF) for x in range(2)]
    slots = lambda v: v.reshape(MAXB, 8, LANES)
    near = []
    for ref in (lo_ref, hi_ref):
        got = ref[HALF * ROWS :, :LANES].astype(F32)
        near.append(jnp.where(got < 0.0, -2.0, got * 8.0 + zrow))

    for x, y, i, k in places:
        halo = (lo_ref, hi_ref)[x][y * ROWS : y * ROWS + ROWS, :]
        row = near[x][HALF * part + y : HALF * part + y + 1]
        pick_rows = (key_ref[i][:, :ROWS] == row[:, :ROWS]).astype(F32).astype(BF16)
        g = jnp.dot(pick_rows, halo, preferred_element_type=F32)
        cx = cen_ref[0, i]
        speed = jnp.abs(LAM * cx + vel_ref[3:4, :LANES])
        step = jnp.where(cx > 0.0, 2.0 * LAM, -2.0 * LAM)
        parts = []
        for at in tiles4:
            parts.append((acc_ref[i, :, at] + speed * g[:, at]).astype(BF16))
            speed = speed + step
        now = jnp.concatenate(parts, axis=1)
        read[k] = now
        sums = jnp.dot(now, wts_ref[...], preferred_element_type=F32)
        total_ref[k] = jnp.sum(slots(sums * fac_ref[i]), axis=0)

    cells = 2 * HALF * 8
    total = total_ref[...].reshape(cells, LANES)
    at = lambda k: total[:, k : k + 1]
    mass = at(0)
    per = 1.0 / mass
    u = [(at(1 + d) + at(4 + d)) * per for d in range(3)]
    energy = at(7) + at(8) + at(9) + at(10) + at(11)
    warm = (energy * per - (u[0] * u[0] + u[1] * u[1] + u[2] * u[2])) / 3.0
    widen = jnp.concatenate([widen_ref[x * 8 + HALF * part : x * 8 + HALF * part + HALF] for x in range(2)], axis=0)
    aim = warm * widen.reshape(cells, LANES)[:, :1]
    rate = 1.0 - jnp.exp(-IMPACT_KIND * (mass / VB) * jnp.sqrt(warm))
    area = 2.0 * math.pi * aim
    scale = rate * mass / (area * jnp.sqrt(area))
    sharp = 0.5 * math.log2(math.e) / aim
    for k, v in enumerate((u[0], u[1], u[2], -sharp, jnp.sqrt(sharp), scale, 1.0 - rate)):
        cell_ref[k] = jnp.broadcast_to(v, (cells, LANES)).reshape(2 * HALF, 8, LANES)

    for x, y, i, k in places:
        ux, uy, uz, fall, root, scale, keep = (cell_ref[q, k][None] for q in range(7))
        off_y = slots(cen_ref[1, i]) - uy + vel_ref[1:2, :LANES][None]
        off_z = slots(cen_ref[2, i]) - uz + vel_ref[2:3, :LANES][None]
        side = (off_y * off_y + off_z * off_z) * fall
        off_x = (slots(cen_ref[0, i]) - ux + vel_ref[:1, :LANES][None]) * root
        step = root + root
        for at in tiles4:
            now = slots(read[k, :, at].astype(F32))
            after = now * keep + scale * jnp.exp2(side - off_x * off_x)
            rows[:, k * 8 : k * 8 + 8, at] = after.astype(BF16)
            off_x = off_x + step

    def put(tile, value):
        where = slice(8 * tile, 8 * tile + 8)
        if part:
            value = value + prev_ref[:, where, :].astype(F32)
        out_ref[:, where, :] = value.astype(BF16)

    sub = iota((16, 8, LANES), 1)
    info = jnp.zeros((16, 4, 8, LANES), F32) if part else prev_ref[...].astype(F32).reshape(16, 4, 8, LANES)
    before = [None] + [info[:, p - 1] for p in range(1, 4)]
    for t in range(3):
        out = jnp.dot(sel_ref[part], rows[4 * t : 4 * t + 4].reshape(256, VB), preferred_element_type=F32)
        out = out.reshape(16, 4, 8, VB)
        for k, at in enumerate(tiles4):
            for p in range(4):
                value = out[:, p, :, at]
                put(12 * p + 4 * t + k, jnp.where(sub >= 2 * p, value, before[p]) if p else value)
                before[p] = value
    put(48, jnp.where(sub >= 6, info[:, 3], before[3]))
    for p in (1, 2):
        where = slice(96 * (p + 1), 96 * (p + 1) + 8)
        value = out_ref[:, where, :].astype(F32) + jnp.where(sub < 2 * p, before[p], 0.0)
        out_ref[:, where, :] = value.astype(BF16)


def unpack_kernel(got_ref, out_ref, ids_ref, cnt_ref, rows, sems):
    row, col = iota((256, 256), 0), iota((256, 256), 1)
    slot, source, rank = row // 64, row % 64 // 2, row % 2
    phase = source % 4
    perm = (col == phase * 64 + source // 4 * 8 + (2 * slot + rank + 2 * phase) % 8).astype(F32).astype(BF16)
    sub = iota((1, 8, LANES), 1)
    upper = [None] + [(sub >= 2 * p).astype(F32).astype(BF16) for p in range(1, 4)]
    lower = [None] + [(sub < 2 * p).astype(F32).astype(BF16) for p in range(1, 4)]
    copies = []
    for t in range(3):
        for g in range(2):
            tile = lambda n: got_ref[8 * g : 8 * g + 8, 8 * n : 8 * n + 8, :]
            lanes = []
            for k in range(4):
                parts = [tile(4 * t + k).reshape(64, LANES)]
                for p in range(1, 4):
                    n = 12 * p + 4 * t + k
                    parts.append((tile(n) * upper[p] + tile(n + 1) * lower[p]).reshape(64, LANES))
                lanes.append(jnp.concatenate(parts, axis=0))
            out = jnp.dot(perm, jnp.concatenate(lanes, axis=1), preferred_element_type=F32)
            where = (pl.ds(4 * t, 4), pl.ds(64 * g, 64))
            rows[where] = out.reshape(4, 64, VB).astype(BF16)
            copies.append(pltpu.make_async_copy(rows.at[where], out_ref.at[where], sems.at[2 * t + g]))
            copies[-1].start()
    place = iota((LANES, 512), 0)
    source, rank = place // 2, place % 2
    phase = source % 4
    pick = (iota((LANES, 512), 1) == phase * 128 + source // 4 * 8 + 2 * phase + rank).astype(F32).astype(BF16)
    meta = jnp.concatenate([got_ref[:, 96 * p : 96 * p + 8, :].reshape(128, LANES) for p in range(1, 5)], axis=0)
    info = jnp.dot(pick, meta, preferred_element_type=F32).T.astype(jnp.int32)
    ids_ref[...] = info[:MAXB].reshape(MAXB, 1, LANES)
    cnt_ref[...] = info[MAXB : MAXB + 1]
    for copy in copies:
        copy.wait()


def call(kernel, outs, scratch=(), flops=0, moved=0, vmem=16 << 20, **extra):
    return pl.pallas_call(
        kernel,
        out_shape=[jax.ShapeDtypeStruct(s, d) for s, d in outs],
        scratch_shapes=list(scratch),
        compiler_params=pltpu.CompilerParams(vmem_limit_bytes=vmem),
        cost_estimate=pl.CostEstimate(flops=flops, bytes_accessed=moved, transcendentals=0),
        **extra,
    )


def tables():
    j = np.arange(VB)
    w = np.stack([j // (BLK * BLK), j // BLK % BLK, j % BLK]).astype(np.float32) - (BLK - 1) / 2.0
    vel = np.zeros((8, VB), np.float32)
    vel[:3] = w
    vel[3:6] = np.float32(LAM) * w
    weights = np.zeros((VB, LANES), np.float32)
    weights[:, [0, 1, 2, 3, 7]] = 1.0
    for d in range(3):
        weights[:, 4 + d] = w[d]
        weights[:, 8 + d] = w[d]
    weights[:, 11] = (w * w).sum(0)
    return vel, weights


def advance(distribution, block_ids, cell_counts, owner, restitution):
    nx, ny, nz = (lax.axis_size(a) for a in ("gx", "gy", "gz"))

    def up(v, axis, n):
        return lax.ppermute(v, axis, [(i, (i + 1) % n) for i in range(n)])

    def down(v, axis, n):
        return lax.ppermute(v, axis, [((i + 1) % n, i) for i in range(n)])

    d = distribution.transpose(0, 1, 3, 2, 4).reshape(TILES, ROWS, VB)
    ids = block_ids.reshape(TILES * 8, MAXB)
    cnt = cell_counts.reshape(TILES, 8)
    own = owner.reshape(TILES, 8)
    rest = restitution.reshape(TILES, 8)
    vel, weights = tables()
    vel, weights = jnp.asarray(vel), jnp.asarray(weights, BF16)

    face_x = ((HALF * ROWS + 8, VB), BF16)
    face_y, face_z = ((2, ROWS + 8, VB), BF16), ((TILES, 16, VB), BF16)
    flat = d.reshape(TILES * ROWS, VB)
    hbm, whole = pl.BlockSpec(memory_space=pltpu.HBM), pl.BlockSpec(memory_space=pltpu.VMEM)
    small = [((TILES * 8, MAXB), jnp.int32), ((TILES, 8), jnp.int32), ((TILES, 8), jnp.int32), ((TILES, 8), BF16)]
    xlo, xhi, ylo, yhi, zlo, zhi, ids, cnt, own, rest = call(
        front_kernel,
        [face_x, face_x, face_y, face_y, face_z, face_z] + small,
        scratch=[pltpu.VMEM((TILES * ROWS, VB), BF16), pltpu.SemaphoreType.DMA((10,))],
        flops=10**8,
        moved=4 * 10**6,
        in_specs=[hbm] * 5,
    )(*(pltpu.with_memory_space_constraint(v, pltpu.HBM) for v in (flat, ids, cnt, own, rest)))
    near_x = [(up(xhi, "gx", nx), down(xlo, "gx", nx))]
    xlo, xhi = call(
        face_kernel,
        [face_x, face_x],
        scratch=[pltpu.SemaphoreType.DMA((2,))],
        moved=2 * 10**6,
        in_specs=[pl.BlockSpec(memory_space=pl.ANY), whole, whole],
    )(flat, ids, cnt)
    near_x.append((up(xhi, "gx", nx), down(xlo, "gx", nx)))
    y_hi, y_lo = down(ylo, "gy", ny), up(yhi, "gy", ny)
    z_hi, z_lo = down(zlo, "gz", nz), up(zhi, "gz", nz)
    (acc,) = call(local_kernel, [((TILES, ROWS, VB), F32)], flops=10**9, moved=6 * 10**6)(
        d, y_lo, y_hi, z_lo, z_hi, ids, cnt, vel
    )
    wide = ((TILES, ROWS, LANES), F32)
    sel, meta, keys, centres, factors, widen = call(
        route_kernel,
        [((2, 512, 256), BF16), ((512, LANES), BF16), wide, ((3, TILES, ROWS, LANES), F32), wide, ((TILES, 8, LANES), F32)],
        flops=10**7,
        moved=10**6,
    )(ids, cnt, own, rest)
    out = meta
    for part in range(2):
        (out,) = call(
            functools.partial(final_kernel, part),
            [((16, 392, LANES), BF16)],
            scratch=[
                pltpu.VMEM((2 * HALF, ROWS, VB), BF16),
                pltpu.VMEM((MAXB, 2 * HALF * 8, VB), BF16),
                pltpu.VMEM((2 * HALF, 8, LANES), F32),
                pltpu.VMEM((7, 2 * HALF, 8, LANES), F32),
            ],
            flops=10**9,
            moved=4 * 10**6,
        )(acc, *near_x[part], keys, centres, factors, widen, vel, weights, sel, out)
    out = out.reshape(64, 49, 2, LANES)
    got = lax.all_to_all(out, ("gx", "gz"), split_axis=0, concat_axis=0, tiled=True).reshape(16, 392, LANES)
    moved, moved_ids, moved_counts = call(
        unpack_kernel,
        [((MAXB, LANES, VB), BF16), ((MAXB, 1, LANES), jnp.int32), ((1, LANES), jnp.int32)],
        scratch=[pltpu.VMEM((MAXB, LANES, VB), BF16), pltpu.SemaphoreType.DMA((6,))],
        flops=4 * 10**8,
        moved=4 * 10**6,
        out_specs=[pl.BlockSpec(memory_space=pl.ANY), whole, whole],
    )(got)
    return (
        moved.transpose(1, 0, 2).reshape(1, LANES, MAXB, VB),
        moved_ids.transpose(1, 2, 0),
        moved_counts,
    )


def solution(mesh):
    placed = (
        P("gx", "gy", "gz", None, None),
        P("gx", "gy", "gz", None),
        P("gx", "gy", "gz"),
        P("gx", "gy", "gz"),
        P("gx", "gy", "gz"),
    )
    return jax.shard_map(
        advance,
        mesh=mesh,
        in_specs=placed,
        out_specs=(
            P("gy", ("gx", "gz"), None, None),
            P("gy", ("gx", "gz"), None),
            P("gy", ("gx", "gz")),
        ),
        check_vma=False,
    )
```

```python
import functools
import math

import jax
import jax.numpy as jnp
import numpy as np
from jax import lax
from jax.experimental import pallas as pl
from jax.experimental.pallas import tpu as pltpu
from jax.sharding import PartitionSpec as P


NV1 = 48
BLK = 8
MAXB = 12
EDGE = NV1 // BLK
VB = BLK**3
TILES = 16
PARTS = ((0, 6), (6, 2))
ROWS = MAXB * 8
LANES = 128
STEP_COEFF = 0.6
IMPACT_KIND = 0.02
FAR = 1.0e6
LAM = STEP_COEFF / (NV1 - 1)
F32 = jnp.float32
BF16 = jnp.bfloat16


def iota(shape, dim):
    return lax.broadcasted_iota(jnp.int32, shape, dim)


def mm(a, b):
    return jnp.dot(a.astype(BF16), b.astype(BF16), preferred_element_type=F32)


def spread(rows):
    pick = (iota((8, LANES), 1) % 8 == iota((8, LANES), 0)).astype(F32)
    return mm(rows.astype(F32), pick)


def centre(b):
    return b.astype(F32) * BLK + ((BLK - 1) / 2.0 - (NV1 - 1) / 2.0)


def listed_rows(ids_ref, cnt_ref):
    slots = (iota((MAXB, LANES), 1) // 8 == iota((MAXB, LANES), 0)).astype(F32)
    wide = mm(ids_ref[...].astype(F32), slots)
    mine = iota((LANES, LANES), 1) % 8 == iota((LANES, LANES), 0) % 8
    ids = jnp.sum(jnp.where(mine, wide, 0.0).reshape(TILES, 8, LANES), axis=1)
    lane = iota((TILES, LANES), 1)
    live = ((lane // 8).astype(F32) < spread(cnt_ref[...])) & (lane < ROWS)
    return ids, live


def x_copies(part, d_ref, outs, sems):
    first, count = PARTS[part]
    copies = []
    for k, out in enumerate(outs):
        source = d_ref.at[pl.ds((8 * k + first) * ROWS, count * ROWS)]
        copies.append(pltpu.make_async_copy(source, out.at[pl.ds(0, count * ROWS)], sems.at[k]))
    return copies


def put_keys(listed, outs):
    start = PARTS[0][1] * ROWS
    for k, out in enumerate(outs):
        out[start:, :LANES] = listed[8 * k : 8 * k + 8].astype(BF16)
        out[start:, LANES:] = jnp.zeros((8, VB - LANES), BF16)


def face_kernel(d_ref, lo, hi, sems):
    copies = x_copies(1, d_ref, (lo, hi), sems)
    for copy in copies:
        copy.start()
    for copy in copies:
        copy.wait()


def front_kernel(d_hbm, ids_hbm, cnt_hbm, own_hbm, rest_hbm, lo, hi, ids_ref, cnt_ref, own_ref, rest_ref, sems):
    pairs = ((ids_hbm, ids_ref), (cnt_hbm, cnt_ref), (own_hbm, own_ref), (rest_hbm, rest_ref))
    small = [pltpu.make_async_copy(a, b, sems.at[2 + n]) for n, (a, b) in enumerate(pairs)]
    large = x_copies(0, d_hbm, (lo, hi), sems)
    for copy in small + large:
        copy.start()
    for copy in small[:2]:
        copy.wait()
    ids, live = listed_rows(ids_ref, cnt_ref)
    put_keys(jnp.where(live, ids, -1.0), (lo, hi))
    for copy in large + small[2:]:
        copy.wait()


def side_kernel(d_ref, ids_ref, cnt_ref, ylo, yhi, zlo, zhi):
    ids, live = listed_rows(ids_ref, cnt_ref)
    listed = jnp.where(live, ids, -1.0)
    lane = iota((TILES, LANES), 1)
    keys = []
    for z, first in ((0, 112), (7, 96)):
        source = iota((LANES, LANES), 0)
        target = iota((LANES, LANES), 1) - first
        move = ((source == target * 8 + z) & (target >= 0) & (target < MAXB)).astype(F32)
        keys.append(jnp.where((lane >= first) & (lane < first + MAXB), mm(listed, move), -1.0))
    row = iota((32, ROWS), 0)
    wanted = jnp.where(row < 16, row * 8, (row - 16) * 8 + 7)
    valid = (row % 16) < MAXB
    select = ((iota((32, ROWS), 1) == wanted) & valid).astype(BF16)
    key_row = iota((16, LANES), 0) == MAXB
    for i in range(TILES):
        tile = d_ref[i]
        if i % 8 in (0, 7):
            out = yhi if i % 8 else ylo
            out[i // 8, :ROWS, :] = tile
            tail = jnp.concatenate([jnp.broadcast_to(listed[i : i + 1], (8, LANES)), jnp.zeros((8, VB - LANES), F32)], axis=1)
            out[i // 8, ROWS:, :] = tail.astype(BF16)
        faces = jnp.dot(select, tile, preferred_element_type=F32)
        for out, start, key in ((zlo, 0, keys[0]), (zhi, 16, keys[1])):
            face = faces[start : start + 16]
            first = jnp.where(key_row, jnp.broadcast_to(key[i : i + 1], (16, LANES)), face[:, :LANES])
            out[i, :, :LANES] = first.astype(BF16)
            out[i, :, LANES:] = face[:, LANES:].astype(BF16)


def local_kernel(d_ref, ylo, yhi, zlo, zhi, ids_ref, cnt_ref, cen_ref, vel_ref, acc_ref):
    ids, live = listed_rows(ids_ref, cnt_ref)
    lane = iota((TILES, LANES), 1)
    tile = iota((TILES, LANES), 0)
    zl = lane % 8
    number = ids.astype(jnp.int32)
    bx, by, bz = number // (EDGE * EDGE), number // EDGE % EDGE, number % EDGE
    half = EDGE // 2
    key = ids * 8.0 + zl.astype(F32)
    none = jnp.full((TILES, LANES), -1.0, F32)
    x_low = tile < 8
    inner = live & ((x_low & (bx < half)) | (jnp.logical_not(x_low) & (bx >= half)))
    z_up = bz >= half
    z_step = jnp.where(z_up, -1.0, 1.0)
    z_edge = (z_up & (zl == 0)) | (jnp.logical_not(z_up) & (zl == 7))
    kz = jnp.where(z_edge, ids + jnp.where(z_up, 4096.0, 8192.0), key + z_step)
    first = jnp.concatenate(
        [
            jnp.where(inner, key, none),
            jnp.where(live & (by >= half), key, none),
            jnp.where(live & (by < half), key, none),
            jnp.where(live, kz, none),
            jnp.zeros((4 * TILES, LANES), F32),
        ],
        axis=0,
    )
    first = first.T
    near = jnp.where(live, key, -2.0)
    zrow = zl[:1].astype(F32)
    one_lane = lane[:1]
    column = lambda which, i: first[:ROWS, which * TILES + i : which * TILES + i + 1]

    def halo_key(ref, x):
        got = ref[x, ROWS:, :LANES].astype(F32)[:1]
        return jnp.where(got < 0.0, -2.0, got * 8.0 + zrow)

    def match(col, row):
        return (col == row).astype(F32).astype(BF16)

    for i in range(TILES):
        x, y = divmod(i, 8)
        own = d_ref[i]
        other = (1 - x) * 8 + y
        gx = jnp.dot(match(column(0, i), near[other : other + 1, :ROWS]), d_ref[other], preferred_element_type=F32)
        low, low_key = (ylo[x, :ROWS, :], halo_key(ylo, x)) if y == 0 else (d_ref[i - 1], near[i - 1 : i])
        high, high_key = (yhi[x, :ROWS, :], halo_key(yhi, x)) if y == 7 else (d_ref[i + 1], near[i + 1 : i + 2])
        gy = jnp.dot(match(column(1, i), low_key[:, :ROWS]), low, preferred_element_type=F32)
        gy = gy + jnp.dot(match(column(2, i), high_key[:, :ROWS]), high, preferred_element_type=F32)
        edge = jnp.maximum(zlo[i, :, :LANES].astype(F32)[MAXB : MAXB + 1], zhi[i, :, :LANES].astype(F32)[MAXB : MAXB + 1])
        edge = jnp.where(edge < 0.0, -2.0, edge + jnp.where(one_lane < 112, 4096.0, 8192.0))
        zkey = jnp.where(one_lane < ROWS, near[i : i + 1], edge)
        around = jnp.concatenate([own, zlo[i], zhi[i]], axis=0)
        gz = jnp.dot(match(column(3, i), zkey), around, preferred_element_type=F32)
        c = [cen_ref[k, i] for k in range(3)]
        speed = [jnp.abs(LAM * c[k] + vel_ref[3 + k : 4 + k, :LANES]) for k in range(3)]
        step = jnp.where(c[0] > 0.0, 2.0 * LAM, -2.0 * LAM)
        real = c[1] < FAR / 2
        for t in range(4):
            at = slice(LANES * t, LANES * t + LANES)
            f = own[:, at].astype(F32)
            acc = f
            for k, g in enumerate((gx, gy, gz)):
                acc = acc + speed[k] * (g[:, at] - f)
            acc_ref[i, :, at] = jnp.where(real, acc, 0.0)
            speed[0] = speed[0] + step


def route_kernel(ids_ref, cnt_ref, own_ref, rest_ref, sel0, sel1, meta_ref, key_ref, cen_ref, fac_ref, widen_ref):
    lane = iota((TILES, LANES), 1)
    here = lane // 8 == iota((TILES, LANES), 0)
    flat = lambda v: jnp.sum(jnp.where(here, spread(v), 0.0), axis=0, keepdims=True)
    owner, count = flat(own_ref[...]), flat(cnt_ref[...])
    sub = iota((LANES, LANES), 0)
    cols = jnp.where(sub == 0, owner, jnp.where(sub == 1, count, 0.0)).T
    earlier = (cols[:, :1] == owner) & (sub < iota((LANES, LANES), 1))
    rank = jnp.sum(earlier.astype(F32), axis=0, keepdims=True)
    home = owner * 8.0 + rank
    for (first, count), out in zip(PARTS, (sel0, sel1)):
        mine = jnp.concatenate([home[:, 64 * x + 8 * first : 64 * x + 8 * (first + count)] for x in range(2)], axis=1)
        mine = mine.astype(jnp.int32)
        shifts = [(mine % 8 + mine // 8 * 2 + 2 * s) % 8 for s in range(4)]
        target = jnp.concatenate([mine // 8 * 8 + shift for shift in shifts], axis=1).astype(F32)
        out[...] = (iota((512, 64 * count), 0).astype(F32) == target).astype(F32).astype(BF16)
    phase = 2 * (owner.astype(jnp.int32) % 4)
    place = (iota((512, LANES), 0).astype(F32) == home + phase.astype(F32)).astype(F32)
    wide = mm(ids_ref[...].astype(F32), (iota((MAXB, LANES), 0) == iota((MAXB, LANES), 1)).astype(F32))
    info = jnp.where(iota((LANES, LANES), 1) == MAXB, cols[:, 1:2], wide)
    meta_ref[...] = mm(place, info).astype(BF16)

    ids, live = listed_rows(ids_ref, cnt_ref)
    number = ids.astype(jnp.int32)
    bx, by, bz = number // (EDGE * EDGE), number // EDGE % EDGE, number % EDGE
    outer = live & (((iota((TILES, LANES), 0) < 8) & (bx >= EDGE // 2)) | ((iota((TILES, LANES), 0) >= 8) & (bx < EDGE // 2)))
    widen = 1.0 + spread(rest_ref[...])
    table = jnp.concatenate(
        [
            jnp.where(outer, ids * 8.0 + (lane % 8).astype(F32), -1.0),
            centre(bx),
            centre(by),
            centre(bz),
            live.astype(F32),
            widen * widen / 4.0,
            jnp.zeros((2 * TILES, LANES), F32),
        ],
        axis=0,
    ).T
    one = iota((1, LANES), 1)
    pick = lambda *pairs: sum((one == at).astype(F32) * value for at, value in pairs)
    plain = pick((0, 1.0), (4, 1.0), (5, 1.0), (6, 1.0), (11, 1.0))
    linear = [pick((1 + d, 1.0), (8 + d, 2.0)) for d in range(3)]
    square = pick((7, 1.0))
    for i in range(TILES):
        wide = lambda which: jnp.broadcast_to(table[:ROWS, which * TILES + i : which * TILES + i + 1], (ROWS, LANES))
        key_ref[i] = wide(0)
        c = [wide(1 + d) for d in range(3)]
        norm = c[0] * c[0] + c[1] * c[1] + c[2] * c[2]
        fac_ref[i] = plain + c[0] * linear[0] + c[1] * linear[1] + c[2] * linear[2] + norm * square
        cen_ref[0, i] = c[0]
        cen_ref[1, i] = jnp.where(wide(4) > 0.0, c[1], FAR)
        cen_ref[2, i] = c[2]
        widen_ref[i] = wide(5)[:8]


def final_kernel(
    part, acc_ref, lo_key, hi_key, lo_ref, hi_ref, key_ref, cen_ref, fac_ref, widen_ref, vel_ref, wts_ref, sel_ref, prev_ref, out_ref,
    read, rows, cell_ref,
):
    zrow = (iota((8, LANES), 1) % 8).astype(F32)
    tiles4 = [slice(LANES * t, LANES * t + LANES) for t in range(4)]
    start, count = PARTS[part]
    slots = lambda v: v.reshape(-1, 8, LANES)
    cells = count * 8
    near = []
    for ref in (lo_key, hi_key):
        got = ref[PARTS[0][1] * ROWS :, :LANES].astype(F32)
        near.append(jnp.where(got < 0.0, -2.0, got * 8.0 + zrow))

    for x in range(2):
        mine = slice(x * count, x * count + count)
        for y in range(count):
            i, k = x * 8 + start + y, x * count + y
            halo = (lo_ref, hi_ref)[x][y * ROWS : y * ROWS + ROWS, :]
            row = near[x][start + y : start + y + 1]
            pick_rows = (key_ref[i][:, :ROWS] == row[:, :ROWS]).astype(F32).astype(BF16)
            g = jnp.dot(pick_rows, halo, preferred_element_type=F32)
            cx = cen_ref[0, i]
            speed = jnp.abs(LAM * cx + vel_ref[3:4, :LANES])
            step = jnp.where(cx > 0.0, 2.0 * LAM, -2.0 * LAM)
            parts = []
            for at in tiles4:
                parts.append((acc_ref[i, :, at] + speed * g[:, at]).astype(BF16))
                speed = speed + step
            read[k] = jnp.concatenate(parts, axis=1)
        sums = jnp.dot(read[mine].reshape(count * ROWS, VB), wts_ref[...], preferred_element_type=F32)
        total = []
        for y in range(count):
            total.append(jnp.sum(slots(sums[y * ROWS : y * ROWS + ROWS] * fac_ref[x * 8 + start + y]), axis=0))
        total = jnp.concatenate(total, axis=0)
        at = lambda k: total[:, k : k + 1]
        mass = at(0)
        per = 1.0 / mass
        u = [(at(1 + d) + at(4 + d)) * per for d in range(3)]
        energy = at(7) + at(8) + at(9) + at(10) + at(11)
        warm = (energy * per - (u[0] * u[0] + u[1] * u[1] + u[2] * u[2])) / 3.0
        widen = widen_ref[x * 8 + start : x * 8 + start + count]
        aim = warm * widen.reshape(cells, LANES)[:, :1]
        rate = 1.0 - jnp.exp(-IMPACT_KIND * (mass / VB) * jnp.sqrt(warm))
        area = 2.0 * math.pi * aim
        scale = rate * mass / (area * jnp.sqrt(area))
        sharp = 0.5 * math.log2(math.e) / aim
        for k, v in enumerate((u[0], u[1], u[2], -sharp, jnp.sqrt(sharp), scale, 1.0 - rate)):
            cell_ref[k, mine] = jnp.broadcast_to(v, (cells, LANES)).reshape(count, 8, LANES)

    def collide(t, x, y):
        i, k = x * 8 + start + y, x * count + y
        some = slice(32 * t, 32 * t + 32)
        ux, uy, uz, fall, root, scale, keep = (cell_ref[q, k][None] for q in range(7))
        off_y = slots(cen_ref[1, i, some]) - uy + vel_ref[1:2, :LANES][None]
        off_z = slots(cen_ref[2, i, some]) - uz + vel_ref[2:3, :LANES][None]
        side = (off_y * off_y + off_z * off_z) * fall
        off_x = (slots(cen_ref[0, i, some]) - ux + vel_ref[:1, :LANES][None]) * root
        step = root + root
        for at in tiles4:
            now = slots(read[k, some, at].astype(F32))
            after = now * keep + scale * jnp.exp2(side - off_x * off_x)
            rows[4 * t : 4 * t + 4, k * 8 : k * 8 + 8, at] = after.astype(BF16)
            off_x = off_x + step

    def put(tile, value):
        where = slice(8 * tile, 8 * tile + 8)
        value = value.astype(BF16)
        out_ref[:, where, :] = value + prev_ref[:, where, :] if part else value

    sub = iota((16, 8, LANES), 1)
    info = jnp.zeros((16, 4, 8, LANES), F32) if part else prev_ref[...].astype(F32).reshape(16, 4, 8, LANES)
    before = [None] + [info[:, p - 1] for p in range(1, 4)]
    for t in range(3):
        for x in range(2):
            for y in range(count):
                collide(t, x, y)
        out = jnp.dot(sel_ref[...], rows[4 * t : 4 * t + 4].reshape(64 * count, VB), preferred_element_type=F32)
        out = out.reshape(16, 4, 8, VB)
        for k, at in enumerate(tiles4):
            for p in range(4):
                value = out[:, p, :, at]
                put(12 * p + 4 * t + k, jnp.where(sub >= 2 * p, value, before[p]) if p else value)
                before[p] = value
    put(48, jnp.where(sub >= 6, info[:, 3], before[3]))
    for p in (1, 2):
        where = slice(96 * (p + 1), 96 * (p + 1) + 8)
        out_ref[:, where, :] = out_ref[:, where, :] + jnp.where(sub < 2 * p, before[p], 0.0).astype(BF16)


def unpack_kernel(got_ref, out_ref, ids_ref, cnt_ref, rows, sems):
    col = iota((1, 256), 1)
    phase, shifted = col // 64, (col % 8 - 2 * (col // 64) + 8) % 8
    source = col % 64 // 8 * 4 + phase
    perm = (iota((256, 256), 0) == shifted // 2 * 64 + source * 2 + shifted % 2).astype(F32).astype(BF16)
    sub = iota((1, 8, LANES), 1)
    upper = [None] + [jnp.broadcast_to((sub >= 2 * p).astype(F32).astype(BF16), (8, 8, LANES)) > 0 for p in range(1, 4)]
    copies = []
    for t in range(3):
        for g in range(2):
            tile = lambda n: got_ref[8 * g : 8 * g + 8, 8 * n : 8 * n + 8, :]
            lanes = []
            for k in range(4):
                parts = [tile(4 * t + k).reshape(64, LANES)]
                for p in range(1, 4):
                    n = 12 * p + 4 * t + k
                    parts.append(jnp.where(upper[p], tile(n), tile(n + 1)).reshape(64, LANES))
                lanes.append(jnp.concatenate(parts, axis=0))
            out = jnp.dot(perm, jnp.concatenate(lanes, axis=1), preferred_element_type=F32)
            where = (pl.ds(4 * t, 4), pl.ds(64 * g, 64))
            rows[where] = out.reshape(4, 64, VB).astype(BF16)
            copies.append(pltpu.make_async_copy(rows.at[where], out_ref.at[where], sems.at[2 * t + g]))
            copies[-1].start()
    col = iota((1, 512), 1)
    phase, at = col // 128, col % 8
    target = jnp.where(at // 2 == phase, (col % 128 // 8 * 4 + phase) * 2 + at % 2, -1)
    pick = (iota((LANES, 512), 0) == target).astype(F32).astype(BF16)
    meta = jnp.concatenate([got_ref[:, 96 * p : 96 * p + 8, :].reshape(128, LANES) for p in range(1, 5)], axis=0)
    info = jnp.dot(pick, meta, preferred_element_type=F32).T.astype(jnp.int32)
    ids_ref[...] = info[:MAXB].reshape(MAXB, 1, LANES)
    cnt_ref[...] = info[MAXB : MAXB + 1]
    for copy in copies:
        copy.wait()


def call(kernel, outs, scratch=(), flops=0, moved=0, vmem=16 << 20, **extra):
    return pl.pallas_call(
        kernel,
        out_shape=[jax.ShapeDtypeStruct(s, d) for s, d in outs],
        scratch_shapes=list(scratch),
        compiler_params=pltpu.CompilerParams(vmem_limit_bytes=vmem),
        cost_estimate=pl.CostEstimate(flops=flops, bytes_accessed=moved, transcendentals=0),
        **extra,
    )


def tables():
    j = np.arange(VB)
    w = np.stack([j // (BLK * BLK), j // BLK % BLK, j % BLK]).astype(np.float32) - (BLK - 1) / 2.0
    vel = np.zeros((8, VB), np.float32)
    vel[:3] = w
    vel[3:6] = np.float32(LAM) * w
    weights = np.zeros((VB, LANES), np.float32)
    weights[:, [0, 1, 2, 3, 7]] = 1.0
    for d in range(3):
        weights[:, 4 + d] = w[d]
        weights[:, 8 + d] = w[d]
    weights[:, 11] = (w * w).sum(0)
    return vel, weights


def advance(distribution, block_ids, cell_counts, owner, restitution):
    nx, ny, nz = (lax.axis_size(a) for a in ("gx", "gy", "gz"))

    def up(v, axis, n):
        return lax.ppermute(v, axis, [(i, (i + 1) % n) for i in range(n)])

    def down(v, axis, n):
        return lax.ppermute(v, axis, [((i + 1) % n, i) for i in range(n)])

    d = distribution.transpose(0, 1, 3, 2, 4).reshape(TILES, ROWS, VB)
    ids = block_ids.reshape(TILES * 8, MAXB)
    cnt = cell_counts.reshape(TILES, 8)
    own = owner.reshape(TILES, 8)
    rest = restitution.reshape(TILES, 8)
    vel, weights = tables()
    vel, weights = jnp.asarray(vel), jnp.asarray(weights, BF16)

    face_x = [((PARTS[0][1] * ROWS + 8, VB), BF16), ((PARTS[1][1] * ROWS, VB), BF16)]
    face_y, face_z = ((2, ROWS + 8, VB), BF16), ((TILES, 16, VB), BF16)
    flat = d.reshape(TILES * ROWS, VB)
    hbm, whole = pl.BlockSpec(memory_space=pltpu.HBM), pl.BlockSpec(memory_space=pltpu.VMEM)
    small = [((TILES * 8, MAXB), jnp.int32), ((TILES, 8), jnp.int32), ((TILES, 8), jnp.int32), ((TILES, 8), BF16)]
    xlo, xhi, ids, cnt, own, rest = call(
        front_kernel,
        [face_x[0]] * 2 + small,
        scratch=[pltpu.SemaphoreType.DMA((6,))],
        moved=2 * 10**6,
        in_specs=[hbm] * 5,
    )(*(pltpu.with_memory_space_constraint(v, pltpu.HBM) for v in (flat, ids, cnt, own, rest)))
    near_x = [(up(xhi, "gx", nx), down(xlo, "gx", nx))]
    ylo, yhi, zlo, zhi = call(side_kernel, [face_y, face_y, face_z, face_z], flops=10**8, moved=4 * 10**6)(d, ids, cnt)
    xlo, xhi = call(
        face_kernel,
        [face_x[1]] * 2,
        scratch=[pltpu.SemaphoreType.DMA((2,))],
        moved=2 * 10**6,
        in_specs=[pl.BlockSpec(memory_space=pl.ANY)],
    )(flat)
    near_x.append((up(xhi, "gx", nx), down(xlo, "gx", nx)))
    y_hi, y_lo = down(ylo, "gy", ny), up(yhi, "gy", ny)
    z_hi, z_lo = down(zlo, "gz", nz), up(zhi, "gz", nz)
    wide = ((TILES, ROWS, LANES), F32)
    *sel, meta, keys, centres, factors, widen = call(
        route_kernel,
        [((512, 64 * count), BF16) for _, count in PARTS]
        + [((512, LANES), BF16), wide, ((3, TILES, ROWS, LANES), F32), wide, ((TILES, 8, LANES), F32)],
        flops=10**7,
        moved=10**6,
    )(ids, cnt, own, rest)
    (acc,) = call(local_kernel, [((TILES, ROWS, VB), F32)], flops=10**9, moved=6 * 10**6)(
        d, y_lo, y_hi, z_lo, z_hi, ids, cnt, centres, vel
    )
    out = meta
    for part, (_, count) in enumerate(PARTS):
        (out,) = call(
            functools.partial(final_kernel, part),
            [((16, 392, LANES), BF16)],
            scratch=[
                pltpu.VMEM((2 * count, ROWS, VB), BF16),
                pltpu.VMEM((MAXB, 2 * count * 8, VB), BF16),
                pltpu.VMEM((7, 2 * count, 8, LANES), F32),
            ],
            flops=10**9,
            moved=4 * 10**6,
        )(acc, *near_x[0], *near_x[part], keys, centres, factors, widen, vel, weights, sel[part], out)
    out = out.reshape(64, 49, 2, LANES)
    got = lax.all_to_all(out, ("gx", "gz"), split_axis=0, concat_axis=0, tiled=True).reshape(16, 392, LANES)
    moved, moved_ids, moved_counts = call(
        unpack_kernel,
        [((MAXB, LANES, VB), BF16), ((MAXB, 1, LANES), jnp.int32), ((1, LANES), jnp.int32)],
        scratch=[pltpu.VMEM((MAXB, LANES, VB), BF16), pltpu.SemaphoreType.DMA((6,))],
        flops=4 * 10**8,
        moved=4 * 10**6,
        out_specs=[pl.BlockSpec(memory_space=pl.ANY), whole, whole],
    )(got)
    return (
        moved.transpose(1, 0, 2).reshape(1, LANES, MAXB, VB),
        moved_ids.transpose(1, 2, 0),
        moved_counts,
    )


def solution(mesh):
    placed = (
        P("gx", "gy", "gz", None, None),
        P("gx", "gy", "gz", None),
        P("gx", "gy", "gz"),
        P("gx", "gy", "gz"),
        P("gx", "gy", "gz"),
    )
    return jax.shard_map(
        advance,
        mesh=mesh,
        in_specs=placed,
        out_specs=(
            P("gy", ("gx", "gz"), None, None),
            P("gy", ("gx", "gz"), None),
            P("gy", ("gx", "gz")),
        ),
        check_vma=False,
    )
```

```python
import functools
import math

import jax
import jax.numpy as jnp
import numpy as np
from jax import lax
from jax.experimental import pallas as pl
from jax.experimental.pallas import tpu as pltpu
from jax.sharding import PartitionSpec as P


NV1 = 48
BLK = 8
MAXB = 12
EDGE = NV1 // BLK
VB = BLK**3
TILES = 16
PARTS = ((0, 6), (6, 2))
ROWS = MAXB * 8
LANES = 128
STEP_COEFF = 0.6
IMPACT_KIND = 0.02
FAR = 1.0e6
LAM = STEP_COEFF / (NV1 - 1)
F32 = jnp.float32
BF16 = jnp.bfloat16


def iota(shape, dim):
    return lax.broadcasted_iota(jnp.int32, shape, dim)


def mm(a, b):
    return jnp.dot(a.astype(BF16), b.astype(BF16), preferred_element_type=F32)


def spread(rows):
    pick = (iota((8, LANES), 1) % 8 == iota((8, LANES), 0)).astype(F32)
    return mm(rows.astype(F32), pick)


def centre(b):
    return b.astype(F32) * BLK + ((BLK - 1) / 2.0 - (NV1 - 1) / 2.0)


def listed_rows(ids_ref, cnt_ref):
    slots = (iota((MAXB, LANES), 1) // 8 == iota((MAXB, LANES), 0)).astype(F32)
    wide = mm(ids_ref[...].astype(F32), slots)
    mine = iota((LANES, LANES), 1) % 8 == iota((LANES, LANES), 0) % 8
    ids = jnp.sum(jnp.where(mine, wide, 0.0).reshape(TILES, 8, LANES), axis=1)
    lane = iota((TILES, LANES), 1)
    live = ((lane // 8).astype(F32) < spread(cnt_ref[...])) & (lane < ROWS)
    return ids, live


def x_copies(part, d_ref, outs, sems):
    first, count = PARTS[part]
    copies = []
    for k, out in enumerate(outs):
        source = d_ref.at[pl.ds((8 * k + first) * ROWS, count * ROWS)]
        copies.append(pltpu.make_async_copy(source, out.at[pl.ds(0, count * ROWS)], sems.at[k]))
    return copies


def put_keys(listed, outs):
    start = PARTS[0][1] * ROWS
    for k, out in enumerate(outs):
        out[start:, :LANES] = listed[8 * k : 8 * k + 8].astype(BF16)
        out[start:, LANES:] = jnp.zeros((8, VB - LANES), BF16)


def face_kernel(d_ref, lo, hi, sems):
    copies = x_copies(1, d_ref, (lo, hi), sems)
    for copy in copies:
        copy.start()
    for copy in copies:
        copy.wait()


def front_kernel(d_hbm, ids_hbm, cnt_hbm, own_hbm, rest_hbm, lo, hi, ids_ref, cnt_ref, own_ref, rest_ref, sems):
    pairs = ((ids_hbm, ids_ref), (cnt_hbm, cnt_ref), (own_hbm, own_ref), (rest_hbm, rest_ref))
    small = [pltpu.make_async_copy(a, b, sems.at[2 + n]) for n, (a, b) in enumerate(pairs)]
    large = x_copies(0, d_hbm, (lo, hi), sems)
    for copy in small + large:
        copy.start()
    for copy in small[:2]:
        copy.wait()
    ids, live = listed_rows(ids_ref, cnt_ref)
    put_keys(jnp.where(live, ids, -1.0), (lo, hi))
    for copy in large + small[2:]:
        copy.wait()


def side_kernel(d_ref, ids_ref, cnt_ref, ylo, yhi, zlo, zhi):
    ids, live = listed_rows(ids_ref, cnt_ref)
    listed = jnp.where(live, ids, -1.0)
    lane = iota((TILES, LANES), 1)
    keys = []
    for z, first in ((0, 112), (7, 96)):
        source = iota((LANES, LANES), 0)
        target = iota((LANES, LANES), 1) - first
        move = ((source == target * 8 + z) & (target >= 0) & (target < MAXB)).astype(F32)
        keys.append(jnp.where((lane >= first) & (lane < first + MAXB), mm(listed, move), -1.0))
    row = iota((32, ROWS), 0)
    wanted = jnp.where(row < 16, row * 8, (row - 16) * 8 + 7)
    valid = (row % 16) < MAXB
    select = ((iota((32, ROWS), 1) == wanted) & valid).astype(BF16)
    key_row = iota((16, LANES), 0) == MAXB
    for i in range(TILES):
        tile = d_ref[i]
        if i % 8 in (0, 7):
            out = yhi if i % 8 else ylo
            out[i // 8, :ROWS, :] = tile
            tail = jnp.concatenate([jnp.broadcast_to(listed[i : i + 1], (8, LANES)), jnp.zeros((8, VB - LANES), F32)], axis=1)
            out[i // 8, ROWS:, :] = tail.astype(BF16)
        faces = jnp.dot(select, tile, preferred_element_type=F32)
        for out, start, key in ((zlo, 0, keys[0]), (zhi, 16, keys[1])):
            face = faces[start : start + 16]
            first = jnp.where(key_row, jnp.broadcast_to(key[i : i + 1], (16, LANES)), face[:, :LANES])
            out[i, :, :LANES] = first.astype(BF16)
            out[i, :, LANES:] = face[:, LANES:].astype(BF16)


def local_kernel(d_ref, ylo, yhi, zlo, zhi, ids_ref, cnt_ref, cen_ref, vel_ref, acc_ref):
    ids, live = listed_rows(ids_ref, cnt_ref)
    lane = iota((TILES, LANES), 1)
    tile = iota((TILES, LANES), 0)
    zl = lane % 8
    number = ids.astype(jnp.int32)
    bx, by, bz = number // (EDGE * EDGE), number // EDGE % EDGE, number % EDGE
    half = EDGE // 2
    key = ids * 8.0 + zl.astype(F32)
    none = jnp.full((TILES, LANES), -1.0, F32)
    x_low = tile < 8
    inner = live & ((x_low & (bx < half)) | (jnp.logical_not(x_low) & (bx >= half)))
    z_up = bz >= half
    z_step = jnp.where(z_up, -1.0, 1.0)
    z_edge = (z_up & (zl == 0)) | (jnp.logical_not(z_up) & (zl == 7))
    kz = jnp.where(z_edge, ids + jnp.where(z_up, 4096.0, 8192.0), key + z_step)
    first = jnp.concatenate(
        [
            jnp.where(inner, key, none),
            jnp.where(live & (by >= half), key, none),
            jnp.where(live & (by < half), key, none),
            jnp.where(live, kz, none),
            jnp.zeros((4 * TILES, LANES), F32),
        ],
        axis=0,
    )
    first = first.T
    near = jnp.where(live, key, -2.0)
    zrow = zl[:1].astype(F32)
    one_lane = lane[:1]
    column = lambda which, i: first[:ROWS, which * TILES + i : which * TILES + i + 1]

    def halo_key(ref, x):
        got = ref[x, ROWS:, :LANES].astype(F32)[:1]
        return jnp.where(got < 0.0, -2.0, got * 8.0 + zrow)

    def match(col, row):
        return (col == row).astype(F32).astype(BF16)

    for i in range(TILES):
        x, y = divmod(i, 8)
        own = d_ref[i]
        other = (1 - x) * 8 + y
        gx = jnp.dot(match(column(0, i), near[other : other + 1, :ROWS]), d_ref[other], preferred_element_type=F32)
        low, low_key = (ylo[x, :ROWS, :], halo_key(ylo, x)) if y == 0 else (d_ref[i - 1], near[i - 1 : i])
        high, high_key = (yhi[x, :ROWS, :], halo_key(yhi, x)) if y == 7 else (d_ref[i + 1], near[i + 1 : i + 2])
        gy = jnp.dot(match(column(1, i), low_key[:, :ROWS]), low, preferred_element_type=F32)
        gy = gy + jnp.dot(match(column(2, i), high_key[:, :ROWS]), high, preferred_element_type=F32)
        edge = jnp.maximum(zlo[i, :, :LANES].astype(F32)[MAXB : MAXB + 1], zhi[i, :, :LANES].astype(F32)[MAXB : MAXB + 1])
        edge = jnp.where(edge < 0.0, -2.0, edge + jnp.where(one_lane < 112, 4096.0, 8192.0))
        zkey = jnp.where(one_lane < ROWS, near[i : i + 1], edge)
        around = jnp.concatenate([own, zlo[i], zhi[i]], axis=0)
        gz = jnp.dot(match(column(3, i), zkey), around, preferred_element_type=F32)
        c = [cen_ref[k, i] for k in range(3)]
        speed = [jnp.abs(LAM * c[k] + vel_ref[3 + k : 4 + k, :LANES]) for k in range(3)]
        step = jnp.where(c[0] > 0.0, 2.0 * LAM, -2.0 * LAM)
        real = c[1] < FAR / 2
        for t in range(4):
            at = slice(LANES * t, LANES * t + LANES)
            f = own[:, at].astype(F32)
            acc = f
            for k, g in enumerate((gx, gy, gz)):
                acc = acc + speed[k] * (g[:, at] - f)
            acc_ref[i, :, at] = jnp.where(real, acc, 0.0)
            speed[0] = speed[0] + step


def route_kernel(ids_ref, cnt_ref, own_ref, rest_ref, sel0, sel1, meta_ref, key_ref, cen_ref, fac_ref, widen_ref):
    lane = iota((TILES, LANES), 1)
    here = lane // 8 == iota((TILES, LANES), 0)
    flat = lambda v: jnp.sum(jnp.where(here, spread(v), 0.0), axis=0, keepdims=True)
    owner, count = flat(own_ref[...]), flat(cnt_ref[...])
    sub = iota((LANES, LANES), 0)
    cols = jnp.where(sub == 0, owner, jnp.where(sub == 1, count, 0.0)).T
    earlier = (cols[:, :1] == owner) & (sub < iota((LANES, LANES), 1))
    rank = jnp.sum(earlier.astype(F32), axis=0, keepdims=True)
    home = owner * 8.0 + rank
    for (first, count), out in zip(PARTS, (sel0, sel1)):
        mine = jnp.concatenate([home[:, 64 * x + 8 * first : 64 * x + 8 * (first + count)] for x in range(2)], axis=1)
        mine = mine.astype(jnp.int32)
        shifts = [(mine % 8 + mine // 8 * 2 + 2 * s) % 8 for s in range(4)]
        target = jnp.concatenate([mine // 8 * 8 + shift for shift in shifts], axis=1).astype(F32)
        out[...] = (iota((512, 64 * count), 0).astype(F32) == target).astype(F32).astype(BF16)
    phase = 2 * (owner.astype(jnp.int32) % 4)
    place = (iota((512, LANES), 0).astype(F32) == home + phase.astype(F32)).astype(F32)
    wide = mm(ids_ref[...].astype(F32), (iota((MAXB, LANES), 0) == iota((MAXB, LANES), 1)).astype(F32))
    info = jnp.where(iota((LANES, LANES), 1) == MAXB, cols[:, 1:2], wide)
    meta_ref[...] = mm(place, info).astype(BF16)

    ids, live = listed_rows(ids_ref, cnt_ref)
    number = ids.astype(jnp.int32)
    bx, by, bz = number // (EDGE * EDGE), number // EDGE % EDGE, number % EDGE
    outer = live & (((iota((TILES, LANES), 0) < 8) & (bx >= EDGE // 2)) | ((iota((TILES, LANES), 0) >= 8) & (bx < EDGE // 2)))
    widen = 1.0 + spread(rest_ref[...])
    table = jnp.concatenate(
        [
            jnp.where(outer, ids * 8.0 + (lane % 8).astype(F32), -1.0),
            centre(bx),
            jnp.where(live, centre(by), FAR),
            centre(bz),
            widen * widen / 4.0,
            jnp.zeros((3 * TILES, LANES), F32),
        ],
        axis=0,
    ).T
    one = iota((1, LANES), 1)
    pick = lambda *pairs: sum((one == at).astype(F32) * value for at, value in pairs)
    plain = pick((0, 1.0), (4, 1.0), (5, 1.0), (6, 1.0), (11, 1.0))
    linear = [pick((1 + d, 1.0), (8 + d, 2.0)) for d in range(3)]
    square = pick((7, 1.0))
    for i in range(TILES):
        column = lambda which, n: jnp.broadcast_to(table[:n, which * TILES + i : which * TILES + i + 1], (n, LANES))
        wide = lambda which: column(which, ROWS)
        key_ref[i] = wide(0)
        c = [wide(1 + d) for d in range(3)]
        norm = c[0] * c[0] + c[1] * c[1] + c[2] * c[2]
        fac_ref[i] = plain + c[0] * linear[0] + c[1] * linear[1] + c[2] * linear[2] + norm * square
        cen_ref[0, i] = c[0]
        cen_ref[1, i] = c[1]
        cen_ref[2, i] = c[2]
        widen_ref[i] = column(4, 8)


def final_kernel(
    part, acc_ref, lo_key, hi_key, lo_ref, hi_ref, key_ref, cen_ref, fac_ref, widen_ref, vel_ref, wts_ref, sel_ref, prev_ref, out_ref,
    read, rows, cell_ref,
):
    zrow = (iota((8, LANES), 1) % 8).astype(F32)
    tiles4 = [slice(LANES * t, LANES * t + LANES) for t in range(4)]
    start, count = PARTS[part]
    slots = lambda v: v.reshape(-1, 8, LANES)
    cells = count * 8
    near = []
    for ref in (lo_key, hi_key):
        got = ref[PARTS[0][1] * ROWS :, :LANES].astype(F32)
        near.append(jnp.where(got < 0.0, -2.0, got * 8.0 + zrow))

    for x in range(2):
        mine = slice(x * count, x * count + count)
        for y in range(count):
            i, k = x * 8 + start + y, x * count + y
            halo = (lo_ref, hi_ref)[x][y * ROWS : y * ROWS + ROWS, :]
            row = near[x][start + y : start + y + 1]
            pick_rows = (key_ref[i][:, :ROWS] == row[:, :ROWS]).astype(F32).astype(BF16)
            g = jnp.dot(pick_rows, halo, preferred_element_type=F32)
            cx = cen_ref[0, i]
            speed = jnp.abs(LAM * cx + vel_ref[3:4, :LANES])
            step = jnp.where(cx > 0.0, 2.0 * LAM, -2.0 * LAM)
            parts = []
            for at in tiles4:
                parts.append((acc_ref[i, :, at] + speed * g[:, at]).astype(BF16))
                speed = speed + step
            read[k] = jnp.concatenate(parts, axis=1)
        sums = jnp.dot(read[mine].reshape(count * ROWS, VB), wts_ref[...], preferred_element_type=F32)
        total = []
        for y in range(count):
            total.append(jnp.sum(slots(sums[y * ROWS : y * ROWS + ROWS] * fac_ref[x * 8 + start + y]), axis=0))
        total = jnp.concatenate(total, axis=0)
        at = lambda k: total[:, k : k + 1]
        mass = at(0)
        per = 1.0 / mass
        u = [(at(1 + d) + at(4 + d)) * per for d in range(3)]
        energy = at(7) + at(8) + at(9) + at(10) + at(11)
        warm = (energy * per - (u[0] * u[0] + u[1] * u[1] + u[2] * u[2])) / 3.0
        widen = widen_ref[x * 8 + start : x * 8 + start + count]
        aim = warm * widen.reshape(cells, LANES)[:, :1]
        rate = 1.0 - jnp.exp(-IMPACT_KIND * (mass / VB) * jnp.sqrt(warm))
        area = 2.0 * math.pi * aim
        scale = rate * mass / (area * jnp.sqrt(area))
        sharp = 0.5 * math.log2(math.e) / aim
        for k, v in enumerate((u[0], u[1], u[2], -sharp, jnp.sqrt(sharp), scale, 1.0 - rate)):
            cell_ref[k, mine] = jnp.broadcast_to(v, (cells, LANES)).reshape(count, 8, LANES)

    def collide(t, x, y):
        i, k = x * 8 + start + y, x * count + y
        some = slice(32 * t, 32 * t + 32)
        ux, uy, uz, fall, root, scale, keep = (cell_ref[q, k][None] for q in range(7))
        off_y = slots(cen_ref[1, i, some]) - uy + vel_ref[1:2, :LANES][None]
        off_z = slots(cen_ref[2, i, some]) - uz + vel_ref[2:3, :LANES][None]
        side = (off_y * off_y + off_z * off_z) * fall
        off_x = (slots(cen_ref[0, i, some]) - ux + vel_ref[:1, :LANES][None]) * root
        step = root + root
        for at in tiles4:
            now = slots(read[k, some, at].astype(F32))
            after = now * keep + scale * jnp.exp2(side - off_x * off_x)
            rows[4 * t : 4 * t + 4, k * 8 : k * 8 + 8, at] = after.astype(BF16)
            off_x = off_x + step

    def put(tile, value):
        where = slice(8 * tile, 8 * tile + 8)
        value = value.astype(BF16)
        out_ref[:, where, :] = value + prev_ref[:, where, :] if part else value

    sub = iota((16, 8, LANES), 1)
    info = jnp.zeros((16, 4, 8, LANES), F32) if part else prev_ref[...].astype(F32).reshape(16, 4, 8, LANES)
    before = [None] + [info[:, p - 1] for p in range(1, 4)]
    for t in range(3):
        for x in range(2):
            for y in range(count):
                collide(t, x, y)
        out = jnp.dot(sel_ref[...], rows[4 * t : 4 * t + 4].reshape(64 * count, VB), preferred_element_type=F32)
        out = out.reshape(16, 4, 8, VB)
        for k, at in enumerate(tiles4):
            for p in range(4):
                value = out[:, p, :, at]
                put(12 * p + 4 * t + k, jnp.where(sub >= 2 * p, value, before[p]) if p else value)
                before[p] = value
    put(48, jnp.where(sub >= 6, info[:, 3], before[3]))
    for p in (1, 2):
        where = slice(96 * (p + 1), 96 * (p + 1) + 8)
        out_ref[:, where, :] = out_ref[:, where, :] + jnp.where(sub < 2 * p, before[p], 0.0).astype(BF16)


def unpack_kernel(got_ref, rows, ids_ref, cnt_ref):
    col = iota((1, 256), 1)
    phase, shifted = col // 64, (col % 8 - 2 * (col // 64) + 8) % 8
    source = col % 64 // 8 * 4 + phase
    perm = (iota((256, 256), 0) == shifted // 2 * 64 + source * 2 + shifted % 2).astype(F32).astype(BF16)
    sub = iota((1, 8, LANES), 1)
    upper = [None] + [jnp.broadcast_to((sub >= 2 * p).astype(F32).astype(BF16), (8, 8, LANES)) > 0 for p in range(1, 4)]
    for t in range(3):
        for g in range(2):
            tile = lambda n: got_ref[8 * g : 8 * g + 8, 8 * n : 8 * n + 8, :]
            lanes = []
            for k in range(4):
                parts = [tile(4 * t + k).reshape(64, LANES)]
                for p in range(1, 4):
                    n = 12 * p + 4 * t + k
                    parts.append(jnp.where(upper[p], tile(n), tile(n + 1)).reshape(64, LANES))
                lanes.append(jnp.concatenate(parts, axis=0))
            out = jnp.dot(perm, jnp.concatenate(lanes, axis=1), preferred_element_type=F32)
            where = (pl.ds(4 * t, 4), pl.ds(64 * g, 64))
            rows[where] = out.reshape(4, 64, VB).astype(BF16)
    col = iota((1, 512), 1)
    phase, at = col // 128, col % 8
    target = jnp.where(at // 2 == phase, (col % 128 // 8 * 4 + phase) * 2 + at % 2, -1)
    pick = (iota((LANES, 512), 0) == target).astype(F32).astype(BF16)
    meta = jnp.concatenate([got_ref[:, 96 * p : 96 * p + 8, :].reshape(128, LANES) for p in range(1, 5)], axis=0)
    info = jnp.dot(pick, meta, preferred_element_type=F32).T.astype(jnp.int32)
    ids_ref[...] = info[:MAXB].reshape(MAXB, 1, LANES)
    cnt_ref[...] = info[MAXB : MAXB + 1]


def call(kernel, outs, scratch=(), flops=0, moved=0, vmem=16 << 20, **extra):
    return pl.pallas_call(
        kernel,
        out_shape=[jax.ShapeDtypeStruct(s, d) for s, d in outs],
        scratch_shapes=list(scratch),
        compiler_params=pltpu.CompilerParams(vmem_limit_bytes=vmem),
        cost_estimate=pl.CostEstimate(flops=flops, bytes_accessed=moved, transcendentals=0),
        **extra,
    )


def tables():
    j = np.arange(VB)
    w = np.stack([j // (BLK * BLK), j // BLK % BLK, j % BLK]).astype(np.float32) - (BLK - 1) / 2.0
    vel = np.zeros((8, VB), np.float32)
    vel[:3] = w
    vel[3:6] = np.float32(LAM) * w
    weights = np.zeros((VB, LANES), np.float32)
    weights[:, [0, 1, 2, 3, 7]] = 1.0
    for d in range(3):
        weights[:, 4 + d] = w[d]
        weights[:, 8 + d] = w[d]
    weights[:, 11] = (w * w).sum(0)
    return vel, weights


def advance(distribution, block_ids, cell_counts, owner, restitution):
    nx, ny, nz = (lax.axis_size(a) for a in ("gx", "gy", "gz"))

    def up(v, axis, n):
        return lax.ppermute(v, axis, [(i, (i + 1) % n) for i in range(n)])

    def down(v, axis, n):
        return lax.ppermute(v, axis, [((i + 1) % n, i) for i in range(n)])

    d = distribution.transpose(0, 1, 3, 2, 4).reshape(TILES, ROWS, VB)
    ids = block_ids.reshape(TILES * 8, MAXB)
    cnt = cell_counts.reshape(TILES, 8)
    own = owner.reshape(TILES, 8)
    rest = restitution.reshape(TILES, 8)
    vel, weights = tables()
    vel, weights = jnp.asarray(vel), jnp.asarray(weights, BF16)

    face_x = [((PARTS[0][1] * ROWS + 8, VB), BF16), ((PARTS[1][1] * ROWS, VB), BF16)]
    face_y, face_z = ((2, ROWS + 8, VB), BF16), ((TILES, 16, VB), BF16)
    flat = d.reshape(TILES * ROWS, VB)
    hbm, whole = pl.BlockSpec(memory_space=pltpu.HBM), pl.BlockSpec(memory_space=pltpu.VMEM)
    small = [((TILES * 8, MAXB), jnp.int32), ((TILES, 8), jnp.int32), ((TILES, 8), jnp.int32), ((TILES, 8), BF16)]
    xlo, xhi, ids, cnt, own, rest = call(
        front_kernel,
        [face_x[0]] * 2 + small,
        scratch=[pltpu.SemaphoreType.DMA((6,))],
        moved=2 * 10**6,
        in_specs=[hbm] * 5,
    )(*(pltpu.with_memory_space_constraint(v, pltpu.HBM) for v in (flat, ids, cnt, own, rest)))
    near_x = [(up(xhi, "gx", nx), down(xlo, "gx", nx))]
    ylo, yhi, zlo, zhi = call(side_kernel, [face_y, face_y, face_z, face_z], flops=10**8, moved=4 * 10**6)(d, ids, cnt)
    xlo, xhi = call(
        face_kernel,
        [face_x[1]] * 2,
        scratch=[pltpu.SemaphoreType.DMA((2,))],
        moved=2 * 10**6,
        in_specs=[pl.BlockSpec(memory_space=pl.ANY)],
    )(flat)
    near_x.append((up(xhi, "gx", nx), down(xlo, "gx", nx)))
    y_hi, y_lo = down(ylo, "gy", ny), up(yhi, "gy", ny)
    z_hi, z_lo = down(zlo, "gz", nz), up(zhi, "gz", nz)
    wide = ((TILES, ROWS, LANES), F32)
    *sel, meta, keys, centres, factors, widen = call(
        route_kernel,
        [((512, 64 * count), BF16) for _, count in PARTS]
        + [((512, LANES), BF16), wide, ((3, TILES, ROWS, LANES), F32), wide, ((TILES, 8, LANES), F32)],
        flops=10**7,
        moved=10**6,
    )(ids, cnt, own, rest)
    (acc,) = call(local_kernel, [((TILES, ROWS, VB), F32)], flops=10**9, moved=6 * 10**6)(
        d, y_lo, y_hi, z_lo, z_hi, ids, cnt, centres, vel
    )
    out = meta
    for part, (_, count) in enumerate(PARTS):
        (out,) = call(
            functools.partial(final_kernel, part),
            [((16, 392, LANES), BF16)],
            scratch=[
                pltpu.VMEM((2 * count, ROWS, VB), BF16),
                pltpu.VMEM((MAXB, 2 * count * 8, VB), BF16),
                pltpu.VMEM((7, 2 * count, 8, LANES), F32),
            ],
            flops=10**9,
            moved=4 * 10**6,
        )(acc, *near_x[0], *near_x[part], keys, centres, factors, widen, vel, weights, sel[part], out)
    out = out.reshape(64, 49, 2, LANES)
    got = lax.all_to_all(out, ("gx", "gz"), split_axis=0, concat_axis=0, tiled=True).reshape(16, 392, LANES)
    moved, moved_ids, moved_counts = call(
        unpack_kernel,
        [((MAXB, LANES, VB), BF16), ((MAXB, 1, LANES), jnp.int32), ((1, LANES), jnp.int32)],
        flops=4 * 10**8,
        moved=4 * 10**6,
    )(got)
    return (
        moved.transpose(1, 0, 2).reshape(1, LANES, MAXB, VB),
        moved_ids.transpose(1, 2, 0),
        moved_counts,
    )


def solution(mesh):
    placed = (
        P("gx", "gy", "gz", None, None),
        P("gx", "gy", "gz", None),
        P("gx", "gy", "gz"),
        P("gx", "gy", "gz"),
        P("gx", "gy", "gz"),
    )
    return jax.shard_map(
        advance,
        mesh=mesh,
        in_specs=placed,
        out_specs=(
            P("gy", ("gx", "gz"), None, None),
            P("gy", ("gx", "gz"), None),
            P("gy", ("gx", "gz")),
        ),
        check_vma=False,
    )
```

```python
import functools
import math

import jax
import jax.numpy as jnp
import numpy as np
from jax import lax
from jax.experimental import pallas as pl
from jax.experimental.pallas import tpu as pltpu
from jax.sharding import PartitionSpec as P


NV1 = 48
BLK = 8
MAXB = 12
EDGE = NV1 // BLK
VB = BLK**3
TILES = 16
PARTS = ((0, 5), (5, 3))
ROWS = MAXB * 8
LANES = 128
STEP_COEFF = 0.6
IMPACT_KIND = 0.02
FAR = 1.0e6
LAM = STEP_COEFF / (NV1 - 1)
F32 = jnp.float32
BF16 = jnp.bfloat16


def iota(shape, dim):
    return lax.broadcasted_iota(jnp.int32, shape, dim)


def mm(a, b):
    return jnp.dot(a.astype(BF16), b.astype(BF16), preferred_element_type=F32)


def spread(rows):
    pick = (iota((8, LANES), 1) % 8 == iota((8, LANES), 0)).astype(F32)
    return mm(rows.astype(F32), pick)


def centre(b):
    return b.astype(F32) * BLK + ((BLK - 1) / 2.0 - (NV1 - 1) / 2.0)


def listed_rows(ids_ref, cnt_ref):
    slots = (iota((MAXB, LANES), 1) // 8 == iota((MAXB, LANES), 0)).astype(F32)
    wide = mm(ids_ref[...].astype(F32), slots)
    mine = iota((LANES, LANES), 1) % 8 == iota((LANES, LANES), 0) % 8
    ids = jnp.sum(jnp.where(mine, wide, 0.0).reshape(TILES, 8, LANES), axis=1)
    lane = iota((TILES, LANES), 1)
    live = ((lane // 8).astype(F32) < spread(cnt_ref[...])) & (lane < ROWS)
    return ids, live


def x_copies(part, d_ref, outs, sems):
    first, count = PARTS[part]
    copies = []
    for k, out in enumerate(outs):
        source = d_ref.at[pl.ds((8 * k + first) * ROWS, count * ROWS)]
        copies.append(pltpu.make_async_copy(source, out.at[pl.ds(0, count * ROWS)], sems.at[k]))
    return copies


def put_keys(listed, outs):
    start = PARTS[0][1] * ROWS
    for k, out in enumerate(outs):
        out[start:, :LANES] = listed[8 * k : 8 * k + 8].astype(BF16)
        out[start:, LANES:] = jnp.zeros((8, VB - LANES), BF16)


def face_kernel(d_ref, lo, hi, sems):
    copies = x_copies(1, d_ref, (lo, hi), sems)
    for copy in copies:
        copy.start()
    for copy in copies:
        copy.wait()


def front_kernel(d_hbm, ids_hbm, cnt_hbm, own_hbm, rest_hbm, lo, hi, ids_ref, cnt_ref, own_ref, rest_ref, sems):
    pairs = ((ids_hbm, ids_ref), (cnt_hbm, cnt_ref), (own_hbm, own_ref), (rest_hbm, rest_ref))
    small = [pltpu.make_async_copy(a, b, sems.at[2 + n]) for n, (a, b) in enumerate(pairs)]
    large = x_copies(0, d_hbm, (lo, hi), sems)
    for copy in small + large:
        copy.start()
    for copy in small[:2]:
        copy.wait()
    ids, live = listed_rows(ids_ref, cnt_ref)
    put_keys(jnp.where(live, ids, -1.0), (lo, hi))
    for copy in large + small[2:]:
        copy.wait()


def side_kernel(d_ref, ids_ref, cnt_ref, ylo, yhi, zlo, zhi):
    ids, live = listed_rows(ids_ref, cnt_ref)
    listed = jnp.where(live, ids, -1.0)
    lane = iota((TILES, LANES), 1)
    keys = []
    for z, first in ((0, 112), (7, 96)):
        source = iota((LANES, LANES), 0)
        target = iota((LANES, LANES), 1) - first
        move = ((source == target * 8 + z) & (target >= 0) & (target < MAXB)).astype(F32)
        keys.append(jnp.where((lane >= first) & (lane < first + MAXB), mm(listed, move), -1.0))
    row = iota((32, ROWS), 0)
    wanted = jnp.where(row < 16, row * 8, (row - 16) * 8 + 7)
    valid = (row % 16) < MAXB
    select = ((iota((32, ROWS), 1) == wanted) & valid).astype(BF16)
    key_row = iota((16, LANES), 0) == MAXB
    for i in range(TILES):
        tile = d_ref[i]
        if i % 8 in (0, 7):
            out = yhi if i % 8 else ylo
            out[i // 8, :ROWS, :] = tile
            tail = jnp.concatenate([jnp.broadcast_to(listed[i : i + 1], (8, LANES)), jnp.zeros((8, VB - LANES), F32)], axis=1)
            out[i // 8, ROWS:, :] = tail.astype(BF16)
        faces = jnp.dot(select, tile, preferred_element_type=F32)
        for out, start, key in ((zlo, 0, keys[0]), (zhi, 16, keys[1])):
            face = faces[start : start + 16]
            first = jnp.where(key_row, jnp.broadcast_to(key[i : i + 1], (16, LANES)), face[:, :LANES])
            out[i, :, :LANES] = first.astype(BF16)
            out[i, :, LANES:] = face[:, LANES:].astype(BF16)


def local_kernel(d_ref, ylo, yhi, zlo, zhi, ids_ref, cnt_ref, cen_ref, vel_ref, acc_ref):
    ids, live = listed_rows(ids_ref, cnt_ref)
    lane = iota((TILES, LANES), 1)
    tile = iota((TILES, LANES), 0)
    zl = lane % 8
    number = ids.astype(jnp.int32)
    bx, by, bz = number // (EDGE * EDGE), number // EDGE % EDGE, number % EDGE
    half = EDGE // 2
    key = ids * 8.0 + zl.astype(F32)
    none = jnp.full((TILES, LANES), -1.0, F32)
    x_low = tile < 8
    inner = live & ((x_low & (bx < half)) | (jnp.logical_not(x_low) & (bx >= half)))
    z_up = bz >= half
    z_step = jnp.where(z_up, -1.0, 1.0)
    z_edge = (z_up & (zl == 0)) | (jnp.logical_not(z_up) & (zl == 7))
    kz = jnp.where(z_edge, ids + jnp.where(z_up, 4096.0, 8192.0), key + z_step)
    first = jnp.concatenate(
        [
            jnp.where(inner, key, none),
            jnp.where(live & (by >= half), key, none),
            jnp.where(live & (by < half), key, none),
            jnp.where(live, kz, none),
            jnp.zeros((4 * TILES, LANES), F32),
        ],
        axis=0,
    )
    first = first.T
    near = jnp.where(live, key, -2.0)
    zrow = zl[:1].astype(F32)
    one_lane = lane[:1]
    column = lambda which, i: first[:ROWS, which * TILES + i : which * TILES + i + 1]

    def halo_key(ref, x):
        got = ref[x, ROWS:, :LANES].astype(F32)[:1]
        return jnp.where(got < 0.0, -2.0, got * 8.0 + zrow)

    def match(col, row):
        return (col == row).astype(F32).astype(BF16)

    for i in range(TILES):
        x, y = divmod(i, 8)
        own = d_ref[i]
        other = (1 - x) * 8 + y
        gx = jnp.dot(match(column(0, i), near[other : other + 1, :ROWS]), d_ref[other], preferred_element_type=F32)
        low, low_key = (ylo[x, :ROWS, :], halo_key(ylo, x)) if y == 0 else (d_ref[i - 1], near[i - 1 : i])
        high, high_key = (yhi[x, :ROWS, :], halo_key(yhi, x)) if y == 7 else (d_ref[i + 1], near[i + 1 : i + 2])
        gy = jnp.dot(match(column(1, i), low_key[:, :ROWS]), low, preferred_element_type=F32)
        gy = gy + jnp.dot(match(column(2, i), high_key[:, :ROWS]), high, preferred_element_type=F32)
        edge = jnp.maximum(zlo[i, :, :LANES].astype(F32)[MAXB : MAXB + 1], zhi[i, :, :LANES].astype(F32)[MAXB : MAXB + 1])
        edge = jnp.where(edge < 0.0, -2.0, edge + jnp.where(one_lane < 112, 4096.0, 8192.0))
        zkey = jnp.where(one_lane < ROWS, near[i : i + 1], edge)
        around = jnp.concatenate([own, zlo[i], zhi[i]], axis=0)
        gz = jnp.dot(match(column(3, i), zkey), around, preferred_element_type=F32)
        c = [cen_ref[k, i] for k in range(3)]
        speed = [jnp.abs(LAM * c[k] + vel_ref[3 + k : 4 + k, :LANES]) for k in range(3)]
        step = jnp.where(c[0] > 0.0, 2.0 * LAM, -2.0 * LAM)
        real = c[1] < FAR / 2
        for t in range(4):
            at = slice(LANES * t, LANES * t + LANES)
            f = own[:, at].astype(F32)
            acc = f
            for k, g in enumerate((gx, gy, gz)):
                acc = acc + speed[k] * (g[:, at] - f)
            acc_ref[i, :, at] = jnp.where(real, acc, 0.0)
            speed[0] = speed[0] + step


def route_kernel(ids_ref, cnt_ref, own_ref, rest_ref, sel0, sel1, meta_ref, key_ref, cen_ref, fac_ref, widen_ref):
    lane = iota((TILES, LANES), 1)
    here = lane // 8 == iota((TILES, LANES), 0)
    flat = lambda v: jnp.sum(jnp.where(here, spread(v), 0.0), axis=0, keepdims=True)
    owner, count = flat(own_ref[...]), flat(cnt_ref[...])
    sub = iota((LANES, LANES), 0)
    cols = jnp.where(sub == 0, owner, jnp.where(sub == 1, count, 0.0)).T
    earlier = (cols[:, :1] == owner) & (sub < iota((LANES, LANES), 1))
    rank = jnp.sum(earlier.astype(F32), axis=0, keepdims=True)
    home = owner * 8.0 + rank
    for (first, count), out in zip(PARTS, (sel0, sel1)):
        mine = jnp.concatenate([home[:, 64 * x + 8 * first : 64 * x + 8 * (first + count)] for x in range(2)], axis=1)
        mine = mine.astype(jnp.int32)
        shifts = [(mine % 8 + mine // 8 * 2 + 2 * s) % 8 for s in range(4)]
        target = jnp.concatenate([mine // 8 * 8 + shift for shift in shifts], axis=1).astype(F32)
        out[...] = (iota((512, 64 * count), 0).astype(F32) == target).astype(F32).astype(BF16)
    phase = 2 * (owner.astype(jnp.int32) % 4)
    place = (iota((512, LANES), 0).astype(F32) == home + phase.astype(F32)).astype(F32)
    wide = mm(ids_ref[...].astype(F32), (iota((MAXB, LANES), 0) == iota((MAXB, LANES), 1)).astype(F32))
    info = jnp.where(iota((LANES, LANES), 1) == MAXB, cols[:, 1:2], wide)
    meta_ref[...] = mm(place, info).astype(BF16)

    ids, live = listed_rows(ids_ref, cnt_ref)
    number = ids.astype(jnp.int32)
    bx, by, bz = number // (EDGE * EDGE), number // EDGE % EDGE, number % EDGE
    outer = live & (((iota((TILES, LANES), 0) < 8) & (bx >= EDGE // 2)) | ((iota((TILES, LANES), 0) >= 8) & (bx < EDGE // 2)))
    widen = 1.0 + spread(rest_ref[...])
    table = jnp.concatenate(
        [
            jnp.where(outer, ids * 8.0 + (lane % 8).astype(F32), -1.0),
            centre(bx),
            jnp.where(live, centre(by), FAR),
            centre(bz),
            widen * widen / 4.0,
            jnp.zeros((3 * TILES, LANES), F32),
        ],
        axis=0,
    ).T
    one = iota((1, LANES), 1)
    pick = lambda *pairs: sum((one == at).astype(F32) * value for at, value in pairs)
    plain = pick((0, 1.0), (4, 1.0), (5, 1.0), (6, 1.0), (11, 1.0))
    linear = [pick((1 + d, 1.0), (8 + d, 2.0)) for d in range(3)]
    square = pick((7, 1.0))
    for i in range(TILES):
        column = lambda which, n: jnp.broadcast_to(table[:n, which * TILES + i : which * TILES + i + 1], (n, LANES))
        wide = lambda which: column(which, ROWS)
        key_ref[i] = wide(0)
        c = [wide(1 + d) for d in range(3)]
        norm = c[0] * c[0] + c[1] * c[1] + c[2] * c[2]
        fac_ref[i] = plain + c[0] * linear[0] + c[1] * linear[1] + c[2] * linear[2] + norm * square
        cen_ref[0, i] = c[0]
        cen_ref[1, i] = c[1]
        cen_ref[2, i] = c[2]
        widen_ref[i] = column(4, 8)


def final_kernel(
    part, acc_ref, lo_key, hi_key, lo_ref, hi_ref, key_ref, cen_ref, fac_ref, widen_ref, vel_ref, wts_ref, sel_ref, prev_ref, out_ref,
    read, rows, cell_ref,
):
    zrow = (iota((8, LANES), 1) % 8).astype(F32)
    tiles4 = [slice(LANES * t, LANES * t + LANES) for t in range(4)]
    start, count = PARTS[part]
    slots = lambda v: v.reshape(-1, 8, LANES)
    cells = count * 8
    near = []
    for ref in (lo_key, hi_key):
        got = ref[PARTS[0][1] * ROWS :, :LANES].astype(F32)
        near.append(jnp.where(got < 0.0, -2.0, got * 8.0 + zrow))

    for x in range(2):
        mine = slice(x * count, x * count + count)
        for y in range(count):
            i, k = x * 8 + start + y, x * count + y
            halo = (lo_ref, hi_ref)[x][y * ROWS : y * ROWS + ROWS, :]
            row = near[x][start + y : start + y + 1]
            pick_rows = (key_ref[i][:, :ROWS] == row[:, :ROWS]).astype(F32).astype(BF16)
            g = jnp.dot(pick_rows, halo, preferred_element_type=F32)
            cx = cen_ref[0, i]
            speed = jnp.abs(LAM * cx + vel_ref[3:4, :LANES])
            step = jnp.where(cx > 0.0, 2.0 * LAM, -2.0 * LAM)
            parts = []
            for at in tiles4:
                parts.append((acc_ref[i, :, at] + speed * g[:, at]).astype(BF16))
                speed = speed + step
            read[k] = jnp.concatenate(parts, axis=1)
        sums = jnp.dot(read[mine].reshape(count * ROWS, VB), wts_ref[...], preferred_element_type=F32)
        total = []
        for y in range(count):
            total.append(jnp.sum(slots(sums[y * ROWS : y * ROWS + ROWS] * fac_ref[x * 8 + start + y]), axis=0))
        total = jnp.concatenate(total, axis=0)
        at = lambda k: total[:, k : k + 1]
        mass = at(0)
        per = 1.0 / mass
        u = [(at(1 + d) + at(4 + d)) * per for d in range(3)]
        energy = at(7) + at(8) + at(9) + at(10) + at(11)
        warm = (energy * per - (u[0] * u[0] + u[1] * u[1] + u[2] * u[2])) * (1.0 / 3.0)
        widen = widen_ref[x * 8 + start : x * 8 + start + count]
        aim = warm * widen.reshape(cells, LANES)[:, :1]
        rate = 1.0 - jnp.exp(-IMPACT_KIND * (mass / VB) * jnp.sqrt(warm))
        narrow = lax.rsqrt(aim)
        root = math.sqrt(0.5 * math.log2(math.e)) * narrow
        scale = rate * (mass * (2.0 * math.pi) ** -1.5) * (narrow * narrow * narrow)
        for k, v in enumerate((u[0], u[1], u[2], -(root * root), root, scale, 1.0 - rate)):
            cell_ref[k, mine] = jnp.broadcast_to(v, (cells, LANES)).reshape(count, 8, LANES)

    def collide(t, x, y):
        i, k = x * 8 + start + y, x * count + y
        some = slice(32 * t, 32 * t + 32)
        ux, uy, uz, fall, root, scale, keep = (cell_ref[q, k][None] for q in range(7))
        off_y = slots(cen_ref[1, i, some]) - uy + vel_ref[1:2, :LANES][None]
        off_z = slots(cen_ref[2, i, some]) - uz + vel_ref[2:3, :LANES][None]
        side = (off_y * off_y + off_z * off_z) * fall
        off_x = (slots(cen_ref[0, i, some]) - ux + vel_ref[:1, :LANES][None]) * root
        step = root + root
        for at in tiles4:
            now = slots(read[k, some, at].astype(F32))
            after = now * keep + scale * jnp.exp2(side - off_x * off_x)
            rows[4 * t : 4 * t + 4, k * 8 : k * 8 + 8, at] = after.astype(BF16)
            off_x = off_x + step

    def put(tile, value):
        where = slice(8 * tile, 8 * tile + 8)
        value = value.astype(BF16)
        out_ref[:, where, :] = value + prev_ref[:, where, :] if part else value

    sub = iota((16, 8, LANES), 1)
    info = jnp.zeros((16, 4, 8, LANES), F32) if part else prev_ref[...].astype(F32).reshape(16, 4, 8, LANES)
    before = [None] + [info[:, p - 1] for p in range(1, 4)]
    for t in range(3):
        for x in range(2):
            for y in range(count):
                collide(t, x, y)
        out = jnp.dot(sel_ref[...], rows[4 * t : 4 * t + 4].reshape(64 * count, VB), preferred_element_type=F32)
        out = out.reshape(16, 4, 8, VB)
        for k, at in enumerate(tiles4):
            for p in range(4):
                value = out[:, p, :, at]
                put(12 * p + 4 * t + k, jnp.where(sub >= 2 * p, value, before[p]) if p else value)
                before[p] = value
    put(48, jnp.where(sub >= 6, info[:, 3], before[3]))
    for p in (1, 2):
        where = slice(96 * (p + 1), 96 * (p + 1) + 8)
        out_ref[:, where, :] = out_ref[:, where, :] + jnp.where(sub < 2 * p, before[p], 0.0).astype(BF16)


def unpack_kernel(got_ref, rows, ids_ref, cnt_ref):
    col = iota((1, 256), 1)
    phase, shifted = col // 64, (col % 8 - 2 * (col // 64) + 8) % 8
    source = col % 64 // 8 * 4 + phase
    perm = (iota((256, 256), 0) == shifted // 2 * 64 + source * 2 + shifted % 2).astype(F32).astype(BF16)
    sub = iota((1, 8, LANES), 1)
    upper = [None] + [jnp.broadcast_to((sub >= 2 * p).astype(F32).astype(BF16), (8, 8, LANES)) > 0 for p in range(1, 4)]
    for t in range(3):
        for g in range(2):
            tile = lambda n: got_ref[8 * g : 8 * g + 8, 8 * n : 8 * n + 8, :]
            lanes = []
            for k in range(4):
                parts = [tile(4 * t + k).reshape(64, LANES)]
                for p in range(1, 4):
                    n = 12 * p + 4 * t + k
                    parts.append(jnp.where(upper[p], tile(n), tile(n + 1)).reshape(64, LANES))
                lanes.append(jnp.concatenate(parts, axis=0))
            out = jnp.dot(perm, jnp.concatenate(lanes, axis=1), preferred_element_type=F32)
            where = (pl.ds(4 * t, 4), pl.ds(64 * g, 64))
            rows[where] = out.reshape(4, 64, VB).astype(BF16)
    col = iota((1, 512), 1)
    phase, at = col // 128, col % 8
    target = jnp.where(at // 2 == phase, (col % 128 // 8 * 4 + phase) * 2 + at % 2, -1)
    pick = (iota((LANES, 512), 0) == target).astype(F32).astype(BF16)
    meta = jnp.concatenate([got_ref[:, 96 * p : 96 * p + 8, :].reshape(128, LANES) for p in range(1, 5)], axis=0)
    info = jnp.dot(pick, meta, preferred_element_type=F32).T.astype(jnp.int32)
    ids_ref[...] = info[:MAXB].reshape(MAXB, 1, LANES)
    cnt_ref[...] = info[MAXB : MAXB + 1]


def call(kernel, outs, scratch=(), flops=0, moved=0, vmem=16 << 20, **extra):
    return pl.pallas_call(
        kernel,
        out_shape=[jax.ShapeDtypeStruct(s, d) for s, d in outs],
        scratch_shapes=list(scratch),
        compiler_params=pltpu.CompilerParams(vmem_limit_bytes=vmem),
        cost_estimate=pl.CostEstimate(flops=flops, bytes_accessed=moved, transcendentals=0),
        **extra,
    )


def tables():
    j = np.arange(VB)
    w = np.stack([j // (BLK * BLK), j // BLK % BLK, j % BLK]).astype(np.float32) - (BLK - 1) / 2.0
    vel = np.zeros((8, VB), np.float32)
    vel[:3] = w
    vel[3:6] = np.float32(LAM) * w
    weights = np.zeros((VB, LANES), np.float32)
    weights[:, [0, 1, 2, 3, 7]] = 1.0
    for d in range(3):
        weights[:, 4 + d] = w[d]
        weights[:, 8 + d] = w[d]
    weights[:, 11] = (w * w).sum(0)
    return vel, weights


def advance(distribution, block_ids, cell_counts, owner, restitution):
    nx, ny, nz = (lax.axis_size(a) for a in ("gx", "gy", "gz"))

    def up(v, axis, n):
        return lax.ppermute(v, axis, [(i, (i + 1) % n) for i in range(n)])

    def down(v, axis, n):
        return lax.ppermute(v, axis, [((i + 1) % n, i) for i in range(n)])

    d = distribution.transpose(0, 1, 3, 2, 4).reshape(TILES, ROWS, VB)
    ids = block_ids.reshape(TILES * 8, MAXB)
    cnt = cell_counts.reshape(TILES, 8)
    own = owner.reshape(TILES, 8)
    rest = restitution.reshape(TILES, 8)
    vel, weights = tables()
    vel, weights = jnp.asarray(vel), jnp.asarray(weights, BF16)

    face_x = [((PARTS[0][1] * ROWS + 8, VB), BF16), ((PARTS[1][1] * ROWS, VB), BF16)]
    face_y, face_z = ((2, ROWS + 8, VB), BF16), ((TILES, 16, VB), BF16)
    flat = d.reshape(TILES * ROWS, VB)
    hbm, whole = pl.BlockSpec(memory_space=pltpu.HBM), pl.BlockSpec(memory_space=pltpu.VMEM)
    small = [((TILES * 8, MAXB), jnp.int32), ((TILES, 8), jnp.int32), ((TILES, 8), jnp.int32), ((TILES, 8), BF16)]
    xlo, xhi, ids, cnt, own, rest = call(
        front_kernel,
        [face_x[0]] * 2 + small,
        scratch=[pltpu.SemaphoreType.DMA((6,))],
        moved=2 * 10**6,
        in_specs=[hbm] * 5,
    )(*(pltpu.with_memory_space_constraint(v, pltpu.HBM) for v in (flat, ids, cnt, own, rest)))
    near_x = [(up(xhi, "gx", nx), down(xlo, "gx", nx))]
    ylo, yhi, zlo, zhi = call(side_kernel, [face_y, face_y, face_z, face_z], flops=10**8, moved=4 * 10**6)(d, ids, cnt)
    xlo, xhi = call(
        face_kernel,
        [face_x[1]] * 2,
        scratch=[pltpu.SemaphoreType.DMA((2,))],
        moved=2 * 10**6,
        in_specs=[pl.BlockSpec(memory_space=pl.ANY)],
    )(flat)
    near_x.append((up(xhi, "gx", nx), down(xlo, "gx", nx)))
    y_hi, y_lo = down(ylo, "gy", ny), up(yhi, "gy", ny)
    z_hi, z_lo = down(zlo, "gz", nz), up(zhi, "gz", nz)
    wide = ((TILES, ROWS, LANES), F32)
    *sel, meta, keys, centres, factors, widen = call(
        route_kernel,
        [((512, 64 * count), BF16) for _, count in PARTS]
        + [((512, LANES), BF16), wide, ((3, TILES, ROWS, LANES), F32), wide, ((TILES, 8, LANES), F32)],
        flops=10**7,
        moved=10**6,
    )(ids, cnt, own, rest)
    (acc,) = call(local_kernel, [((TILES, ROWS, VB), F32)], flops=10**9, moved=6 * 10**6)(
        d, y_lo, y_hi, z_lo, z_hi, ids, cnt, centres, vel
    )
    out = meta
    for part, (_, count) in enumerate(PARTS):
        (out,) = call(
            functools.partial(final_kernel, part),
            [((16, 392, LANES), BF16)],
            scratch=[
                pltpu.VMEM((2 * count, ROWS, VB), BF16),
                pltpu.VMEM((MAXB, 2 * count * 8, VB), BF16),
                pltpu.VMEM((7, 2 * count, 8, LANES), F32),
            ],
            flops=10**9,
            moved=4 * 10**6,
        )(acc, *near_x[0], *near_x[part], keys, centres, factors, widen, vel, weights, sel[part], out)
    out = out.reshape(64, 49, 2, LANES)
    got = lax.all_to_all(out, ("gx", "gz"), split_axis=0, concat_axis=0, tiled=True).reshape(16, 392, LANES)
    moved, moved_ids, moved_counts = call(
        unpack_kernel,
        [((MAXB, LANES, VB), BF16), ((MAXB, 1, LANES), jnp.int32), ((1, LANES), jnp.int32)],
        flops=4 * 10**8,
        moved=4 * 10**6,
    )(got)
    return (
        moved.transpose(1, 0, 2).reshape(1, LANES, MAXB, VB),
        moved_ids.transpose(1, 2, 0),
        moved_counts,
    )


def solution(mesh):
    placed = (
        P("gx", "gy", "gz", None, None),
        P("gx", "gy", "gz", None),
        P("gx", "gy", "gz"),
        P("gx", "gy", "gz"),
        P("gx", "gy", "gz"),
    )
    return jax.shard_map(
        advance,
        mesh=mesh,
        in_specs=placed,
        out_specs=(
            P("gy", ("gx", "gz"), None, None),
            P("gy", ("gx", "gz"), None),
            P("gy", ("gx", "gz")),
        ),
        check_vma=False,
    )
```
